32 devices in a mesh: dp: 8 (over z, x), expert: 4 (over y, core).
Axes of the slice: x: 2, y: 2, z: 4, core: 2. Of those that a mesh axis runs over, the one named last changes fastest.
Arguments:
- tokens: bfloat16 [4, 1024, 2048], P('expert', 'dp'), may hold values from -6 to 6
- cotangent: bfloat16 [4, 1024, 2048], P('expert', 'dp'), may hold values from -6 to 6
- lengths: int32 [4], replicated, may hold values from 256 to 1024, as said below
- routes: int32 [4, 1024, 4], P('expert', 'dp'), may hold values from 0 to 7, all different within a row; in each aligned block of 128 rows (0 to 127, 128 to 255, ..., all dimensions but the last counted through in order) at most 80 rows name the same one
- query_weight: bfloat16 [2048, 2048], P(('dp', 'expert')), may hold values from -0.1875 to 0.1875
- key_weight: bfloat16 [2048, 2048], P(('dp', 'expert')), may hold values from -0.1875 to 0.1875
- value_weight: bfloat16 [2048, 2048], P(('dp', 'expert')), may hold values from -0.125 to 0.125
- output_weight: bfloat16 [2048, 2048], P(('dp', 'expert')), may hold values from -0.75 to 0.75
- query_bias: bfloat16 [2048], P(('dp', 'expert')), may hold values from -1.1953125 to 1.1953125
- key_bias: bfloat16 [2048], P(('dp', 'expert')), may hold values from -1.1953125 to 1.1953125
- value_bias: bfloat16 [2048], P(('dp', 'expert')), may hold values from -1.1953125 to 1.1953125
- attention_gain: bfloat16 [2048], P(('dp', 'expert')), may hold values from 0.5 to 1.5
- router_weight: bfloat16 [2048, 8], P(('dp', 'expert')), may hold values from -0.0625 to 0.0625
- shared_switch: bfloat16 [2048], P(('dp', 'expert')), may hold values from -0.125 to 0.125
- mixer_gain: bfloat16 [2048], P(('dp', 'expert')), may hold values from 0.5 to 1.5
- shared_gate_weight: bfloat16 [2048, 5632], P(('dp', 'expert')), may hold values from -0.125 to 0.125
- shared_up_weight: bfloat16 [2048, 5632], P(('dp', 'expert')), may hold values from -0.125 to 0.125
- shared_down_weight: bfloat16 [2048, 5632], P(('dp', 'expert')), may hold values from -0.15625 to 0.15625
- expert_gate: bfloat16 [8, 2048, 1408], P('expert', 'dp'), may hold values from -0.125 to 0.125
- expert_up: bfloat16 [8, 2048, 1408], P('expert', 'dp'), may hold values from -0.125 to 0.125
- expert_down: bfloat16 [8, 2048, 1408], P('expert', 'dp'), may hold values from -0.625 to 0.625
Outputs:
- layer_out: bfloat16 [4, 1024, 2048], P('expert', 'dp')
- balance_loss: float32 [1], replicated
- grad_tokens: bfloat16 [4, 1024, 2048], P('expert', 'dp')
- grad_query_weight: float32 [2048, 2048], P(('dp', 'expert'))
- grad_key_weight: float32 [2048, 2048], P(('dp', 'expert'))
- grad_value_weight: float32 [2048, 2048], P(('dp', 'expert'))
- grad_output_weight: float32 [2048, 2048], P(('dp', 'expert'))
- grad_query_bias: float32 [2048], P(('dp', 'expert'))
- grad_key_bias: float32 [2048], P(('dp', 'expert'))
- grad_value_bias: float32 [2048], P(('dp', 'expert'))
- grad_attention_gain: float32 [2048], P(('dp', 'expert'))
- grad_router_weight: float32 [2048, 8], P(('dp', 'expert'))
- grad_shared_switch: float32 [2048], P(('dp', 'expert'))
- grad_mixer_gain: float32 [2048], P(('dp', 'expert'))
- grad_shared_gate_weight: float32 [2048, 5632], P(('dp', 'expert'))
- grad_shared_up_weight: float32 [2048, 5632], P(('dp', 'expert'))
- grad_shared_down_weight: float32 [2048, 5632], P(('dp', 'expert'))
- grad_expert_gate: float32 [8, 2048, 1408], P('expert', 'dp')
- grad_expert_up: float32 [8, 2048, 1408], P('expert', 'dp')
- grad_expert_down: float32 [8, 2048, 1408], P('expert', 'dp')
The draws below stay inside these ranges and needn't reach their ends.
Inputs may be any that keep to these rules, and one draw needn't show every extreme that they name: Sequence s has lengths[s] valid slots at its start, the rest is padding; one sequence is full at 1024. The 4 experts of a slot differ. In the rows of one device (aligned blocks of 128 slots) no expert is named more than 80 times, and in some block one is named exactly 80 times. Padding slots carry routes too; they are not used.
All inputs are finite; a program needn't handle non-finite values.
Results may differ from the reference program's by a relative error of at most 0.023.
Values may be sent and summed in bfloat16 or wider, within the bound.
No kernel may reach another device: no remote copies, remote signals or barrier semaphores. Data moves between devices by JAX's collectives and lax.ppermute only.
A program may use at most 640 MiB of HBM per device.

```python
import math
import jax
import jax.numpy as jnp
import numpy as np
from jax import lax

D = 2048
HEADS = 16
HD = 128
FFE = 1408
FS = 5632
TOP = 4
TOK_DEV = 128
EXPERTS = 8
LEN = 1024
SEQS = 4
MOST = 80


def draw_lengths(key, part):
    first_key, second_key = jax.random.split(jax.random.fold_in(key, 11))
    lengths_drawn = jax.random.randint(first_key, (SEQS,), LEN // 4, LEN + 1)
    longest_one = jax.random.randint(second_key, (), 0, SEQS)
    return jnp.where(jnp.arange(SEQS) == longest_one, LEN, lengths_drawn).astype(jnp.int32)


def shard_levels(rng, dims, pieces, smallest, top_value):
    level = 1.0
    for axis_at, blocks in pieces:
        heights = jax.random.uniform(jax.random.fold_in(jax.random.fold_in(rng, 6), axis_at), (blocks,), jnp.float32, smallest / len(pieces), top_value / len(pieces))
        level = level * jnp.repeat(jnp.exp(heights), dims[axis_at] // blocks).reshape((-1,) + (1,) * (len(dims) - 1 - axis_at))
    return level


def assign_block(rng, own, number, rows, amount, top, limit, skew):
    ranking = jax.random.permutation(rng, amount)
    crowded, ordinary = shares(amount, rows * top, limit, skew, True), shares(amount, rows * top, limit, skew, False)
    places = jnp.arange(amount)

    def named(sizes, turn):
        used = int((sizes > 0).sum())
        fixed = max(1, used // 4)
        passed = fixed + (places - fixed + turn * (used - fixed)) % max(1, amount - fixed)
        return jnp.zeros((amount,), jnp.int32).at[ranking[jnp.where(places < fixed, places, passed)]].set(jnp.asarray(sizes, jnp.int32))

    sizes = jnp.where(number % 4 == 0, named(crowded, number // 4), named(ordinary, number - number // 4 - 1))
    mixed = jax.random.permutation(jax.random.fold_in(own, 3), amount)
    giver, receiver = mixed[0:amount // 2 * 2:2], mixed[1:amount // 2 * 2:2]
    margin = jnp.minimum(sizes[giver] - 1, limit - sizes[receiver]) // 2
    margin = jnp.where((giver == ranking[0]) | (receiver == ranking[0]) | (sizes[receiver] == 0), 0, jnp.maximum(margin, 0))
    passed = jax.random.randint(jax.random.fold_in(own, 4), (amount // 2,), 0, 1 << 20) % (margin + 1)
    sizes = sizes.at[giver].add(-passed).at[receiver].add(passed)
    members = jnp.searchsorted(jnp.cumsum(sizes), jnp.arange(rows * top), side="right").astype(jnp.int32)
    listing = members.reshape(top, rows).T
    listing = listing[jax.random.permutation(jax.random.fold_in(own, 1), rows)]
    turn = jax.random.randint(jax.random.fold_in(own, 2), (rows, 1), 0, top)
    return jnp.take_along_axis(listing, (jnp.arange(top)[None, :] + turn) % top, axis=1)


def shares(number_of, total, reach, lean, full):
    portions = [(1 << 20) // math.isqrt(standing ** lean) + 1 for standing in range(1, number_of + 1)]
    largest = reach if full else min(reach, max(-(-total // number_of), total * portions[0] // sum(portions)))
    least = 1 if total - largest >= number_of - 1 else 0
    given, rest = [largest] + [least] * (number_of - 1), total - largest - least * (number_of - 1)
    while rest > 0:
        free = [i for i in range(1, number_of) if given[i] < largest] or [i for i in range(1, number_of) if given[i] < reach]
        whole, budget = sum([portions[i] for i in free]), rest
        for i in free:
            more = min(reach - given[i], max(1, budget * portions[i] // whole), rest)
            given[i] = given[i] + more
            rest = rest - more
    return np.array(given)


def centred(rng, dims, spread, most, pieces=(), kind=jnp.bfloat16):
    array = spread * jax.random.normal(rng, dims, jnp.float32)
    if pieces:
        array = array * shard_levels(rng, dims, pieces, -0.22, 0.18)
    return jnp.clip(array, -most, most).astype(kind)


def setup_inputs(seed: int = 0) -> dict:
    streams_of = jax.random.split(jax.random.key(seed), 22)
    tokens = centred(streams_of[0], (SEQS, LEN, D), 1.0, 6.0, ((0, 4), (1, 8)))
    cotangent = centred(streams_of[1], (SEQS, LEN, D), 1.0, 6.0, ((0, 4), (1, 8)))
    lengths = draw_lengths(jax.random.fold_in(streams_of[21], 71), 0)
    routes_keys = jax.random.split(jax.random.fold_in(streams_of[3], 1), SEQS * LEN // TOK_DEV)
    routes_turns = jax.random.permutation(jax.random.fold_in(streams_of[3], 3), SEQS * LEN // TOK_DEV)
    routes = jax.vmap(lambda own, number: assign_block(jax.random.fold_in(streams_of[3], 2), own, number, TOK_DEV, EXPERTS, TOP, MOST, 2))(routes_keys, routes_turns).reshape((SEQS, LEN, TOP))
    query_weight = centred(streams_of[4], (D, D), (D // 2) ** -0.5, 0.1875, ((0, 32),))
    key_weight = centred(streams_of[5], (D, D), (D // 2) ** -0.5, 0.1875, ((0, 32),))
    value_weight = centred(streams_of[6], (D, D), D ** -0.5, 0.125, ((0, 32),))
    output_weight = centred(streams_of[7], (D, D), (D // 32) ** -0.5, 0.75, ((0, 32),))
    query_bias = centred(streams_of[8], (D,), 0.2, 1.1953125, ((0, 32),))
    key_bias = centred(streams_of[9], (D,), 0.2, 1.1953125, ((0, 32),))
    value_bias = centred(streams_of[10], (D,), 0.2, 1.1953125, ((0, 32),))
    attention_gain = jnp.clip(1.0 + 0.1 * jax.random.normal(streams_of[11], (D,), jnp.float32), 0.5, 1.5).astype(jnp.bfloat16)
    router_weight = centred(streams_of[12], (D, EXPERTS), (4 * D) ** -0.5, 0.0625, ((0, 32),))
    shared_switch = centred(streams_of[13], (D,), D ** -0.5, 0.125, ((0, 32),))
    mixer_gain = jnp.clip(1.0 + 0.1 * jax.random.normal(streams_of[14], (D,), jnp.float32), 0.5, 1.5).astype(jnp.bfloat16)
    shared_gate_weight = centred(streams_of[15], (D, FS), D ** -0.5, 0.125, ((0, 32),))
    shared_up_weight = centred(streams_of[16], (D, FS), D ** -0.5, 0.125, ((0, 32),))
    shared_down_weight = centred(streams_of[17], (D, FS), (FS // 4) ** -0.5, 0.15625, ((0, 32),))
    expert_gate = centred(streams_of[18], (EXPERTS, D, FFE), D ** -0.5, 0.125, ((0, 4), (1, 8)))
    expert_up = centred(streams_of[19], (EXPERTS, D, FFE), D ** -0.5, 0.125, ((0, 4), (1, 8)))
    expert_down = centred(streams_of[20], (EXPERTS, D, FFE), (FFE // 16) ** -0.5, 0.625, ((0, 4), (1, 8)))
    return dict(tokens=tokens, cotangent=cotangent, lengths=lengths, routes=routes, query_weight=query_weight, key_weight=key_weight, value_weight=value_weight, output_weight=output_weight, query_bias=query_bias, key_bias=key_bias, value_bias=value_bias, attention_gain=attention_gain, router_weight=router_weight, shared_switch=shared_switch, mixer_gain=mixer_gain, shared_gate_weight=shared_gate_weight, shared_up_weight=shared_up_weight, shared_down_weight=shared_down_weight, expert_gate=expert_gate, expert_up=expert_up, expert_down=expert_down)


@jax.custom_vjp
def low(v):
    return lax.optimization_barrier(v.astype(jnp.bfloat16)).astype(jnp.float32)

@jax.custom_vjp
def low_back(v):
    return v

def low_keep(v):
    return (low(v), None)

def low_pass(kept, grad):
    return (grad,)

def back_keep(v):
    return (v, None)

def back_low(kept, grad):
    return (low(grad),)
low.defvjp(low_keep, low_pass)
low_back.defvjp(back_keep, back_low)
epsilon = 1e-06
rope_base = 1000000.0
highest = lax.Precision.HIGHEST
neg_large = -1e+30

def matmul(left, right):
    return jnp.dot(left, right, precision=highest)

def rope_tables(positions, head_width):
    halfway = head_width // 2
    freqs = rope_base ** (-jnp.arange(halfway, dtype=jnp.float32) * 2.0 / head_width)
    angles = positions.astype(jnp.float32)[:, None] * freqs[None, :]
    angles = jnp.concatenate([angles, angles], axis=1)
    return (jnp.cos(angles), jnp.sin(angles))

def rotate(values, cosine, sine):
    halfway = values.shape[-1] // 2
    turned = jnp.concatenate([-values[..., halfway:], values[..., :halfway]], axis=-1)
    return values * cosine[:, None, :] + turned * sine[:, None, :]

def attend_sequence(queries, keys, values, length):
    block_rows = min(512, LEN)
    starts = (jnp.arange(LEN // block_rows) * block_rows).astype(jnp.int32)
    blocks = queries.reshape(LEN // block_rows, block_rows, HEADS, HD)
    key_pos = jnp.arange(LEN)

    def one_block(block_pair):
        query_rows, first_row = block_pair
        scores = jnp.einsum('qhd,khd->hqk', query_rows, keys, precision=highest) * HD ** (-0.5)
        scores = low_back(scores)
        query_pos = first_row + jnp.arange(block_rows)
        allowed = (key_pos[None, :] <= query_pos[:, None]) & (key_pos[None, :] < length)
        scores = jnp.where(allowed[None], scores, neg_large)
        attn_weights = jax.nn.softmax(scores, axis=-1)
        return jnp.einsum('hqk,khd->qhd', low(attn_weights), values, precision=highest)
    outputs = lax.map(jax.checkpoint(one_block), (blocks, starts))
    return outputs.reshape(LEN, HEADS, HD)

def expert_branch(rows, gate_w, up_w, down_w):
    entering = low_back(rows)
    gate_pre = low_back(matmul(entering, gate_w))
    up_pre = low_back(matmul(entering, up_w))
    hidden = low(jax.nn.silu(gate_pre) * up_pre)
    return low(low_back(jnp.dot(hidden, down_w.T, precision=highest)))

def forward(token_rows, weight_list, routes, lengths):
    query_weight, key_weight, value_weight, output_weight, query_bias, key_bias, value_bias, attention_gain, router_weight, shared_switch, mixer_gain, shared_gate_weight, shared_up_weight, shared_down_weight, expert_gate, expert_up, expert_down = weight_list
    positions = jnp.arange(LEN)
    live = (positions[None, :] < lengths[:, None]).astype(jnp.float32)
    attn_inv = lax.rsqrt(lax.optimization_barrier(jnp.mean(token_rows * token_rows, axis=-1, keepdims=True)) + epsilon)
    normed_attn = low(token_rows * attn_inv * attention_gain)
    query_pre = low_back(matmul(normed_attn, query_weight) + query_bias)
    key_pre = low_back(matmul(normed_attn, key_weight) + key_bias)
    value_pre = low_back(matmul(normed_attn, value_weight) + value_bias)
    cosine, sine = rope_tables(positions, HD)
    queries = low(rotate(query_pre.reshape(SEQS, LEN, HEADS, HD), cosine, sine))
    keys = low(rotate(key_pre.reshape(SEQS, LEN, HEADS, HD), cosine, sine))
    values = low(value_pre.reshape(SEQS, LEN, HEADS, HD))
    mixed = jax.vmap(attend_sequence)(queries, keys, values, lengths)
    mixed = low(low_back(mixed.reshape(SEQS, LEN, D)))
    resid = token_rows + low_back(matmul(mixed, output_weight))
    mix_inv = lax.rsqrt(lax.optimization_barrier(jnp.mean(resid * resid, axis=-1, keepdims=True)) + epsilon)
    normed_mix = low(resid * mix_inv * mixer_gain)
    logits = low_back(matmul(normed_mix, router_weight))
    probs = jax.nn.softmax(logits, axis=-1)
    chosen = (routes[..., None] == jnp.arange(EXPERTS)).astype(jnp.float32) * live[..., None, None]
    gate_weight = lax.optimization_barrier(jnp.sum(chosen, axis=2)) * probs
    routed = jnp.zeros((SEQS, LEN, D), jnp.float32)
    for expert_index in range(EXPERTS):
        branch_out = jax.checkpoint(expert_branch)(normed_mix, expert_gate[expert_index], expert_up[expert_index], expert_down[expert_index])
        routed = routed + gate_weight[..., expert_index:expert_index + 1] * branch_out
    switch = jax.nn.sigmoid(matmul(normed_mix, shared_switch))
    shared_gate_pre = low_back(matmul(normed_mix, shared_gate_weight))
    shared_up_pre = low_back(matmul(normed_mix, shared_up_weight))
    shared_hidden = low(jax.nn.silu(shared_gate_pre) * shared_up_pre)
    shared_out = low_back(jnp.dot(shared_hidden, shared_down_weight.T, precision=highest))
    layer_out = (resid + routed + switch[..., None] * shared_out) * live[..., None]
    counts = lax.optimization_barrier(jnp.sum(chosen, axis=(0, 1, 2)))
    total = SEQS * LEN * 1.0
    mass = lax.optimization_barrier(jnp.sum(probs * live[..., None], axis=(0, 1)))
    balance_loss = EXPERTS * jnp.sum(counts / (TOP * total) * mass / total)
    return (layer_out, balance_loss.reshape(1))

def reference(tokens, cotangent, lengths, routes, query_weight, key_weight, value_weight, output_weight, query_bias, key_bias, value_bias, attention_gain, router_weight, shared_switch, mixer_gain, shared_gate_weight, shared_up_weight, shared_down_weight, expert_gate, expert_up, expert_down):
    weight_list = tuple((item.astype(jnp.float32) for item in (query_weight, key_weight, value_weight, output_weight, query_bias, key_bias, value_bias, attention_gain, router_weight, shared_switch, mixer_gain, shared_gate_weight, shared_up_weight, shared_down_weight, expert_gate, expert_up, expert_down)))

    def wrapped(token_rows, *weights_in):
        return forward(token_rows, weights_in, routes, lengths)
    (layer_out, balance_loss), pullback = jax.vjp(wrapped, tokens.astype(jnp.float32), *weight_list)
    grads = pullback((cotangent.astype(jnp.float32), jnp.ones((1,), jnp.float32)))
    return (layer_out.astype(jnp.bfloat16), balance_loss, grads[0].astype(jnp.bfloat16), grads[1], grads[2], grads[3], grads[4], grads[5], grads[6], grads[7], grads[8], grads[9], grads[10], grads[11], grads[12], grads[13], grads[14], grads[15], grads[16], grads[17])
```

```python
import jax
import jax.numpy as jnp
from jax import lax
from jax.sharding import PartitionSpec as P

HEADS = 16
HD = 128
LANES = 128
PLANES = 4
PAIR = 2

f32 = jnp.float32
bf16 = jnp.bfloat16

epsilon = 1e-06
rope_base = 1000000.0
highest = lax.Precision.HIGHEST
neg_large = -1e30


def mm(left, right, contract=((1,), (0,))):
    return lax.dot_general(left, right, (contract, ((), ())), preferred_element_type=f32)


def mm_t(left, right):
    return mm(left, right, ((1,), (1,)))


def t_mm(left, right):
    return mm(left, right, ((0,), (0,)))


def rope_tables(positions, head_width):
    halfway = head_width // 2
    freqs = rope_base ** (-jnp.arange(halfway, dtype=f32) * 2.0 / head_width)
    angles = positions.astype(f32)[:, None] * freqs[None, :]
    angles = jnp.concatenate([angles, angles], axis=1)
    return (jnp.cos(angles), jnp.sin(angles))


def rotate(values, cosine, sine):
    halfway = values.shape[-1] // 2
    turned = jnp.concatenate([-values[..., halfway:], values[..., :halfway]], axis=-1)
    return values * cosine[:, None, :] + turned * sine[:, None, :]


def rotate_back(grads_in, cosine, sine):
    halfway = grads_in.shape[-1] // 2
    scaled = grads_in * sine[:, None, :]
    turned = jnp.concatenate([scaled[..., halfway:], -scaled[..., :halfway]], axis=-1)
    return grads_in * cosine[:, None, :] + turned


def norm_back(grad_normed, rows_in, inverse, gain):
    weighted = grad_normed * gain
    inner = jnp.sum(weighted * rows_in, axis=-1, keepdims=True)
    grad_rows = inverse * weighted - rows_in * inverse**3 * inner / rows_in.shape[-1]
    grad_gain = jnp.sum(grad_normed * rows_in * inverse, axis=0)
    return (grad_rows, grad_gain)


def add_low(*parts):
    total = parts[0].astype(f32)
    for part in parts[1:]:
        total = total + part.astype(f32)
    return total.astype(bf16)


class Links:
    def __init__(self, dp_size, expert_size):
        self.planes = PLANES
        self.across = dp_size // PLANES
        self.rows = expert_size // PAIR
        self.sizes = dict(z=PLANES, x=self.across, y=self.rows, c=PAIR)
        self.total = dp_size * expert_size
        dp_index = lax.axis_index("dp")
        expert_index = lax.axis_index("expert")
        self.at = dict(
            z=dp_index // self.across,
            x=dp_index % self.across,
            y=expert_index // PAIR,
            c=expert_index % PAIR,
        )

    def place(self, index):
        c = index % PAIR
        y = index // PAIR % self.rows
        x = index // (PAIR * self.rows) % self.across
        z = index // (PAIR * self.rows * self.across)
        return dict(z=z, x=x, y=y, c=c)

    def index(self, where):
        return (
            (where["z"] * self.across + where["x"]) * self.rows + where["y"]
        ) * PAIR + where["c"]

    def send(self, value, target):
        pairs = []
        for source in range(self.total):
            goal = target(self.place(source))
            if goal is not None:
                pairs.append((source, self.index(goal)))
        return lax.ppermute(value, ("dp", "expert"), pairs)

    def turn(self, value, axis, steps):
        size = self.sizes[axis]
        return self.send(value, lambda w: {**w, axis: (w[axis] + steps) % size})

    def swap(self, value, axis, bit):
        return self.send(value, lambda w: {**w, axis: w[axis] ^ bit})

    def step(self, value, steps, lowest, highest_at):
        return self.send(
            value,
            lambda w: {**w, "z": w["z"] + steps} if lowest <= w["z"] <= highest_at else None,
        )

    def behind(self, axis, steps):
        return (self.at[axis] - steps) % self.sizes[axis]

    def ahead(self, axis, steps):
        return (self.at[axis] + steps) % self.sizes[axis]

    def gather_z(self, value):
        return [value] + [self.turn(value, "z", s) for s in range(1, PLANES)]

    def scatter_z(self, blocks):
        got = [self.turn(blocks[s], "z", -s) for s in range(1, PLANES)]
        return [blocks[0]] + got

    def gather_x(self, value):
        return [value] + [self.turn(value, "x", t) for t in range(1, self.across)]

    def place_rows(self, blocks, axis, dim):
        shape = blocks[0].shape[:dim] + (self.sizes[axis],) + blocks[0].shape[dim:]
        buffer = jnp.zeros(shape, blocks[0].dtype)
        for s, block in enumerate(blocks):
            buffer = lax.dynamic_update_slice_in_dim(
                buffer, jnp.expand_dims(block, dim), self.behind(axis, s), dim
            )
        return buffer

    def pick(self, value, index, dim):
        return lax.dynamic_index_in_dim(value, index, dim, keepdims=False)

    def reduce_all(self, value):
        for axis in ("c", "y", "x", "z"):
            bit = 1
            while bit < self.sizes[axis]:
                value = value + self.swap(value, axis, bit)
                bit *= 2
        return value

    def scatter_axis(self, value, axis, dim):
        total = self.pick(value, self.at[axis], dim).astype(f32)
        for s in range(1, self.sizes[axis]):
            total = total + self.turn(
                self.pick(value, self.ahead(axis, s), dim), axis, s
            ).astype(f32)
        return total


def per_device(
    tokens,
    cotangent,
    lengths,
    routes,
    query_weight,
    key_weight,
    value_weight,
    output_weight,
    query_bias,
    key_bias,
    value_bias,
    attention_gain,
    router_weight,
    shared_switch,
    mixer_gain,
    shared_gate_weight,
    shared_up_weight,
    shared_down_weight,
    expert_gate,
    expert_up,
    expert_down,
):
    dp_size = lax.axis_size("dp")
    groups = lax.axis_size("expert")
    net = Links(dp_size, groups)
    across, yrows = net.across, net.rows
    rows = tokens.shape[1]
    width = tokens.shape[2]
    top_count = routes.shape[2]
    local_experts = expert_gate.shape[0]
    num_experts = local_experts * groups
    units = local_experts + 1
    inner = expert_gate.shape[2]
    weight_rows = expert_gate.shape[1]
    shard = query_weight.shape[0]
    head_cols = width // PLANES
    heads = head_cols // HD
    window = -(-inner // (PLANES * LANES)) * LANES
    scale = HD ** (-0.5)
    all_slots = float(groups * rows * dp_size)
    iz, ix, iy, ic = net.at["z"], net.at["x"], net.at["y"], net.at["c"]
    expert_at = lax.axis_index("expert")

    tok = tokens.reshape(rows, width)
    cot = cotangent.reshape(rows, width)
    length = jnp.take(lengths, expert_at)
    own_start = lax.axis_index("dp") * rows
    positions = own_start + jnp.arange(rows)
    valid = positions < length
    live = valid.astype(f32)[:, None]
    token_rows = tok.astype(f32)
    grad_final = cot.astype(f32) * live

    tok_blocks = net.gather_z(tok)
    extras = jnp.concatenate(
        [
            attention_gain[:, None],
            mixer_gain[:, None],
            shared_switch[:, None],
            router_weight,
            jnp.zeros((shard, LANES - 3 - num_experts), bf16),
        ],
        axis=1,
    )

    def head_slice(goal):
        return jnp.concatenate(
            [
                lax.dynamic_slice_in_dim(w, goal * head_cols, head_cols, 1)
                for w in (query_weight, key_weight, value_weight)
            ]
            + [extras],
            axis=1,
        )

    qkv_blocks = [
        head_slice(iz) if s == 0 else net.turn(head_slice(net.ahead("z", s)), "z", s)
        for s in range(PLANES)
    ]
    qkv_w = net.place_rows(qkv_blocks, "z", 0)
    qkv_w = net.place_rows(net.gather_x(qkv_w), "x", 1)
    qkv_w = net.place_rows([qkv_w, net.turn(qkv_w, "y", 1)], "y", 2)
    qkv_w = net.place_rows([qkv_w, net.turn(qkv_w, "c", 1)], "c", 3)
    qkv_w = qkv_w.reshape(width, 3 * head_cols + LANES)
    small = qkv_w[:, 3 * head_cols :]
    qkv_w = qkv_w[:, : 3 * head_cols]
    attn_gain_f = small[:, 0].astype(f32)
    mixer_gain_f = small[:, 1].astype(f32)
    switch_full = small[:, 2]
    router_full = small[:, 3 : 3 + num_experts]

    biases = jnp.concatenate(
        [
            query_bias[:, None],
            key_bias[:, None],
            value_bias[:, None],
            jnp.zeros((shard, LANES - 3), bf16),
        ],
        axis=1,
    )
    out_w = jnp.concatenate([output_weight, biases], axis=1)
    out_w = net.place_rows(net.gather_x(out_w), "x", 0)
    out_w = net.place_rows([out_w, net.turn(out_w, "y", 1)], "y", 1)
    out_w = net.place_rows([out_w, net.turn(out_w, "c", 1)], "c", 2)
    out_w = out_w.reshape(head_cols, width + LANES)
    bias_cols = out_w[:, width : width + 3].astype(f32)
    out_w = out_w[:, :width]
    qkv_bias = jnp.concatenate([bias_cols[:, 0], bias_cols[:, 1], bias_cols[:, 2]])

    def start_of(goal):
        return jnp.minimum(goal * window, inner - window)

    shared_stack = [
        w.reshape(shard, groups, inner)
        for w in (shared_gate_weight, shared_up_weight, shared_down_weight)
    ]

    def shared_for(dy, dc):
        goal = net.ahead("y", dy) * PAIR + net.ahead("c", dc)
        return jnp.stack([net.pick(w, goal, 1) for w in shared_stack])

    shared_rows = jnp.zeros((3, groups, shard, inner), bf16)
    for dy in range(yrows):
        for dc in range(PAIR):
            block = shared_for(dy, dc)
            if dy or dc:
                block = net.send(
                    block,
                    lambda w, dy=dy, dc=dc: {
                        **w,
                        "y": (w["y"] + dy) % yrows,
                        "c": (w["c"] + dc) % PAIR,
                    },
                )
            origin = net.behind("y", dy) * PAIR + net.behind("c", dc)
            shared_rows = lax.dynamic_update_slice_in_dim(
                shared_rows, block[:, None], origin, 1
            )
    shared_rows = shared_rows.reshape(3, groups * shard, inner)
    gate_set = [expert_gate[j] for j in range(local_experts)] + [shared_rows[0]]
    up_set = [expert_up[j] for j in range(local_experts)] + [shared_rows[1]]
    down_set = [expert_down[j] for j in range(local_experts)] + [shared_rows[2]]

    def spread(arrays):
        wide = len(arrays) * window
        full = jnp.zeros((PLANES, across, weight_rows, wide), bf16)
        for s in range(PLANES):
            goal = start_of(net.ahead("z", s))
            block = jnp.concatenate(
                [lax.dynamic_slice_in_dim(w, goal, window, 1) for w in arrays], axis=1
            )
            if s:
                block = net.turn(block, "z", s)
            for t, piece in enumerate(net.gather_x(block)):
                full = lax.dynamic_update_slice(
                    full, piece[None, None], (net.behind("z", s), net.behind("x", t), 0, 0)
                )
        return full.reshape(width, wide)

    def gather_group(value):
        blocks = net.gather_z(value)
        blocks = [[b, net.turn(b, "y", 1)] for b in blocks]
        flat = [b for pair in blocks for b in pair]
        both = jnp.stack(flat)
        other = net.turn(both, "c", 1)
        return jnp.concatenate([both, other], axis=0).reshape(-1, value.shape[1])

    def scatter_group(value, size):
        parts = value.reshape(2, PLANES, yrows, size, -1)
        kept = []
        for s in (1, 2, 3, 0):
            pair = parts[0, s].astype(f32) + net.turn(parts[1, s], "c", 1).astype(f32)
            pair = pair.astype(bf16)
            one = add_low(pair[0], net.turn(pair[1], "y", 1))
            kept.append(net.turn(one, "z", -s) if s else one)
        total = kept[0].astype(f32)
        for part in kept[1:]:
            total = total + part.astype(f32)
        return total

    cot_group = gather_group(cot)
    down_w = spread(down_set)
    gate_w = spread(gate_set)
    up_w = spread(up_set)

    hidden_rows = jnp.concatenate(tok_blocks, axis=0)
    hidden_f = hidden_rows.astype(f32)
    attn_inv_group = lax.rsqrt(jnp.mean(hidden_f * hidden_f, axis=-1, keepdims=True) + epsilon)
    normed_attn = (hidden_f * attn_inv_group * attn_gain_f).astype(bf16)
    qkv_pre = mm(normed_attn, qkv_w) + qkv_bias
    query_pos = jnp.concatenate(
        [
            (net.behind("z", s) * across + ix) * rows + jnp.arange(rows)
            for s in range(PLANES)
        ]
    )
    group_rows = PLANES * rows
    cosine, sine = rope_tables(query_pos, HD)
    queries = rotate(
        qkv_pre[:, :head_cols].reshape(group_rows, heads, HD), cosine, sine
    ).astype(bf16)
    keys_own = (
        rotate(
            qkv_pre[:, head_cols : 2 * head_cols].reshape(group_rows, heads, HD), cosine, sine
        )
        .astype(bf16)
        .reshape(group_rows, head_cols)
    )
    values_own = qkv_pre[:, 2 * head_cols :].astype(bf16)
    keys_values = net.gather_x(jnp.concatenate([keys_own, values_own], axis=1))
    key_pos = jnp.concatenate(
        [query_pos + (net.behind("x", t) - ix) * rows for t in range(across)]
    )
    all_kv = jnp.concatenate(keys_values, axis=0)
    keys_all = all_kv[:, :head_cols].reshape(-1, heads, HD)
    values_all = all_kv[:, head_cols:].reshape(-1, heads, HD)
    scores = jnp.einsum("qhd,khd->hqk", queries, keys_all, preferred_element_type=f32) * scale
    allowed = (key_pos[None, :] <= query_pos[:, None]) & (key_pos[None, :] < length)
    scores = jnp.where(allowed[None], scores, neg_large)
    attn_weights = jax.nn.softmax(scores, axis=-1)
    weights_low = attn_weights.astype(bf16)
    mixed = jnp.einsum("hqk,khd->qhd", weights_low, values_all, preferred_element_type=f32)
    mixed = mixed.astype(bf16).reshape(group_rows, head_cols)
    branch = mm(mixed, out_w).astype(bf16).reshape(PLANES, rows, width)
    resid = token_rows
    for part in net.scatter_z([branch[s] for s in range(PLANES)]):
        resid = resid + part.astype(f32)

    mix_inv = lax.rsqrt(jnp.mean(resid * resid, axis=-1, keepdims=True) + epsilon)
    normed_mix = (resid * mix_inv * mixer_gain_f).astype(bf16)
    logits = mm(normed_mix, router_full)
    probs = jax.nn.softmax(logits, axis=-1)
    route_ids = routes.reshape(rows, top_count)
    chosen = (route_ids[:, :, None] == jnp.arange(num_experts)[None, None, :]) & valid[
        :, None, None
    ]
    chosen_any = jnp.sum(chosen.astype(f32), axis=1)
    gates = probs * chosen_any
    switch = jax.nn.sigmoid(mm(normed_mix, switch_full[:, None]))
    gate_columns = jnp.concatenate([gates, switch * live], axis=1)
    gate_high = lax.reduce_precision(gate_columns, 8, 7)
    gate_rest = gate_columns - gate_high
    gate_count = num_experts + 1
    payload = jnp.concatenate(
        [
            normed_mix,
            gate_high.astype(bf16),
            gate_rest.astype(bf16),
            jnp.zeros((rows, LANES - 2 * gate_count), bf16),
        ],
        axis=1,
    )
    mix_group = gather_group(payload)
    gate_group = mix_group[:, width : width + 2 * gate_count].astype(f32)
    gate_group = gate_group[:, :gate_count] + gate_group[:, gate_count:]
    mix_group = mix_group[:, :width]
    counts = jnp.sum(chosen_any, axis=0)
    mass = jnp.sum(probs * live, axis=0)
    sums = net.reduce_all(jnp.concatenate([counts, mass]).reshape(1, -1))[0]
    fraction = sums[:num_experts] / (top_count * all_slots)
    balance_loss = (
        num_experts * jnp.sum(fraction * sums[num_experts:] / all_slots)
    ).reshape(1)

    unit_gates = jnp.concatenate(
        [
            lax.dynamic_slice_in_dim(gate_group, expert_at * local_experts, local_experts, 1),
            gate_group[:, num_experts:],
        ],
        axis=1,
    )
    column = jnp.arange(window)
    fresh = (column + start_of(iz) >= iz * window).astype(f32)
    wide_gate = (unit_gates[:, :, None] * fresh[None, None, :]).reshape(-1, units * window)
    fresh_wide = jnp.tile(fresh, units)
    grad_hid = mm(cot_group, down_w)
    gate_pre = mm(mix_group, gate_w)
    up_pre = mm(mix_group, up_w)
    sigma = jax.nn.sigmoid(gate_pre)
    act = gate_pre * sigma
    hidden = act * up_pre
    hidden_gated = (hidden * wide_gate).astype(bf16)
    gated_grad = grad_hid * wide_gate
    grad_gate_pre = (gated_grad * up_pre * sigma * (1.0 + gate_pre * (1.0 - sigma))).astype(bf16)
    grad_up_pre = (gated_grad * act).astype(bf16)
    unit_grads = jnp.sum(
        (hidden * grad_hid * fresh_wide).reshape(-1, units, window), axis=2
    )
    out_group = mm_t(hidden_gated, down_w).astype(bf16)
    grad_in = (mm_t(grad_gate_pre, gate_w) + mm_t(grad_up_pre, up_w)).astype(bf16)
    spot = (
        jnp.arange(num_experts)[None, :] == (expert_at * local_experts + jnp.arange(local_experts))[:, None]
    ).astype(f32)
    expert_grads = jnp.sum(unit_grads[:, :local_experts, None] * spot[None], axis=1)
    grad_payload = jnp.concatenate(
        [
            grad_in,
            expert_grads.astype(bf16),
            unit_grads[:, local_experts:].astype(bf16),
            jnp.zeros((grad_in.shape[0], LANES - gate_count), bf16),
        ],
        axis=1,
    )
    grad_sum = scatter_group(grad_payload, rows)
    grad_gates = grad_sum[:, width : width + num_experts]
    grad_switch = grad_sum[:, width + num_experts : width + gate_count]

    grad_switch_logit = grad_switch * live * switch * (1.0 - switch)
    grad_probs = grad_gates * chosen_any * live + live * (num_experts * fraction / all_slots)[None, :]
    grad_logits = (
        probs * (grad_probs - jnp.sum(probs * grad_probs, axis=1, keepdims=True))
    ).astype(bf16)
    grad_normed_mix = (
        grad_sum[:, :width]
        + grad_switch_logit * switch_full.astype(f32)[None, :]
        + mm_t(grad_logits, router_full)
    )
    grad_mix_rows, grad_mixer_gain = norm_back(grad_normed_mix, resid, mix_inv, mixer_gain_f)
    grad_resid = grad_final + grad_mix_rows
    grad_branch = grad_resid.astype(bf16)
    branch_group = jnp.concatenate(net.gather_z(grad_branch), axis=0)

    grad_mixed = mm_t(branch_group, out_w).astype(bf16).reshape(group_rows, heads, HD)
    grad_attn = jnp.einsum("qhd,khd->hqk", grad_mixed, values_all, preferred_element_type=f32)
    delta = jnp.sum(attn_weights * grad_attn, axis=-1, keepdims=True)
    grad_scores = (attn_weights * (grad_attn - delta)).astype(bf16)
    grad_keys = (
        jnp.einsum("hqk,qhd->khd", grad_scores, queries, preferred_element_type=f32) * scale
    )
    grad_values = jnp.einsum("hqk,qhd->khd", weights_low, grad_mixed, preferred_element_type=f32)
    grad_kv = jnp.concatenate(
        [grad_keys.reshape(-1, head_cols), grad_values.reshape(-1, head_cols)], axis=1
    ).reshape(across, group_rows, 2 * head_cols)
    grad_kv_own = grad_kv[0]
    for t in range(1, across):
        grad_kv_own = grad_kv_own + net.turn(grad_kv[t].astype(bf16), "x", -t).astype(f32)
    grad_queries = (
        jnp.einsum("hqk,khd->qhd", grad_scores, keys_all, preferred_element_type=f32) * scale
    )
    grad_query_pre = (
        rotate_back(grad_queries, cosine, sine).reshape(group_rows, head_cols).astype(bf16)
    )
    grad_key_pre = (
        rotate_back(grad_kv_own[:, :head_cols].reshape(group_rows, heads, HD), cosine, sine)
        .reshape(group_rows, head_cols)
        .astype(bf16)
    )
    grad_value_pre = grad_kv_own[:, head_cols:].astype(bf16)
    grad_qkv = jnp.concatenate([grad_query_pre, grad_key_pre, grad_value_pre], axis=1)
    grad_normed_part = mm_t(grad_qkv, qkv_w)
    gain_part = jnp.sum(grad_normed_part * hidden_f * attn_inv_group, axis=0)
    normed_part_low = grad_normed_part.astype(bf16).reshape(PLANES, rows, width)
    grad_normed_attn = jnp.zeros((rows, width), f32)
    for part in net.scatter_z([normed_part_low[s] for s in range(PLANES)]):
        grad_normed_attn = grad_normed_attn + part.astype(f32)
    attn_inv = attn_inv_group[:rows]
    grad_attn_rows, _ = norm_back(grad_normed_attn, token_rows, attn_inv, attn_gain_f)
    grad_tokens = (grad_resid + grad_attn_rows).astype(bf16).reshape(1, rows, width)

    out_sum = scatter_group(out_group, rows)
    layer_out = ((resid + out_sum) * live).astype(bf16)

    def unspread(grad_full):
        wide = grad_full.shape[1]
        blocks = grad_full.astype(bf16).reshape(PLANES, across, weight_rows, wide)
        mine = net.scatter_axis(blocks, "x", 1).astype(bf16)
        got = [
            net.turn(net.pick(mine, net.ahead("z", s), 0), "z", s) if s else net.pick(mine, iz, 0)
            for s in range(PLANES)
        ]
        by_plane = net.place_rows(got, "z", 0)
        result = []
        for j in range(units):
            cols = [by_plane[k, :, j * window : (j + 1) * window] for k in range(PLANES)]
            used = window * (PLANES - 1)
            cols[-1] = cols[-1][:, window - (inner - used) :]
            result.append(jnp.concatenate(cols, axis=1))
        return result

    grads_down = unspread(t_mm(cot_group, hidden_gated))
    grads_gate = unspread(t_mm(mix_group, grad_gate_pre))
    grads_up = unspread(t_mm(mix_group, grad_up_pre))
    grad_expert_gate = jnp.stack(grads_gate[:local_experts]).astype(f32)
    grad_expert_up = jnp.stack(grads_up[:local_experts]).astype(f32)
    grad_expert_down = jnp.stack(grads_down[:local_experts]).astype(f32)
    shared_parts = jnp.stack(
        [g[local_experts].reshape(groups, shard, inner) for g in (grads_gate, grads_up, grads_down)]
    )
    shared_grads = jnp.zeros((3, groups, shard, inner), bf16)
    for dy in range(yrows):
        for dc in range(PAIR):
            goal = net.ahead("y", dy) * PAIR + net.ahead("c", dc)
            block = net.pick(shared_parts, goal, 1)
            if dy or dc:
                block = net.send(
                    block,
                    lambda w, dy=dy, dc=dc: {
                        **w,
                        "y": (w["y"] + dy) % yrows,
                        "c": (w["c"] + dc) % PAIR,
                    },
                )
            origin = net.behind("y", dy) * PAIR + net.behind("c", dc)
            shared_grads = lax.dynamic_update_slice_in_dim(
                shared_grads, block[:, None], origin, 1
            )
    shared_grads = jnp.concatenate(
        [shared_grads[:, g] for g in range(groups)], axis=2
    ).astype(f32)

    def to_rows(part, dims):
        part = net.scatter_axis(part, "c", dims - 1).astype(bf16)
        part = net.scatter_axis(part, "y", dims - 2).astype(bf16)
        return net.scatter_axis(part, "x", dims - 3)

    grad_out_w = t_mm(mixed, branch_group).astype(bf16)
    grad_output_weight = to_rows(
        grad_out_w.reshape(across, yrows, PAIR, shard, width), 3
    )
    grad_qkv_w = t_mm(normed_attn, grad_qkv).astype(bf16)
    qkv_rows = to_rows(
        grad_qkv_w.reshape(PLANES, across, yrows, PAIR, shard, 3 * head_cols), 4
    ).astype(bf16)
    qkv_got = [
        net.turn(net.pick(qkv_rows, net.ahead("z", s), 0), "z", s)
        if s
        else net.pick(qkv_rows, iz, 0)
        for s in range(PLANES)
    ]
    qkv_planes = net.place_rows(qkv_got, "z", 0)
    grad_qkv_weights = [
        jnp.concatenate(
            [qkv_planes[k, :, j * head_cols : (j + 1) * head_cols] for k in range(PLANES)], axis=1
        ).astype(f32)
        for j in range(3)
    ]

    grad_router = t_mm(normed_mix, grad_logits)
    grad_switch_full = jnp.sum(grad_switch_logit * normed_mix.astype(f32), axis=0)

    def spread_sum(part):
        part = net.scatter_axis(part, "c", 3)
        part = net.scatter_axis(part, "y", 2)
        part = net.scatter_axis(part, "x", 1)
        return net.scatter_axis(part, "z", 0)

    early = jnp.concatenate(
        [grad_router.T, grad_switch_full[None], grad_mixer_gain[None]], axis=0
    )
    early = early.reshape(num_experts + 2, PLANES, across, yrows, PAIR, shard)
    early = spread_sum(jnp.transpose(early, (1, 2, 3, 4, 0, 5)))
    grad_router_shard = early[:num_experts].T
    gain_shard = spread_sum(gain_part.reshape(PLANES, across, yrows, PAIR, 1, shard))[0]
    bias_part = jnp.sum(grad_qkv.astype(f32), axis=0).reshape(3, across, yrows, PAIR, shard)
    bias_part = jnp.transpose(bias_part, (1, 2, 3, 0, 4))
    bias_part = net.scatter_axis(bias_part, "c", 2)
    bias_part = net.scatter_axis(bias_part, "y", 1)
    bias_part = net.scatter_axis(bias_part, "x", 0)
    return (
        layer_out.reshape(1, rows, width),
        balance_loss,
        grad_tokens,
        grad_qkv_weights[0],
        grad_qkv_weights[1],
        grad_qkv_weights[2],
        grad_output_weight,
        bias_part[0],
        bias_part[1],
        bias_part[2],
        gain_shard,
        grad_router_shard,
        early[num_experts],
        early[num_experts + 1],
        shared_grads[0],
        shared_grads[1],
        shared_grads[2],
        grad_expert_gate,
        grad_expert_up,
        grad_expert_down,
    )


def solution(mesh):
    rows = P("expert", "dp", None)
    shard2 = P(("dp", "expert"), None)
    shard1 = P(("dp", "expert"))
    owned = P("expert", "dp", None)
    placed = (
        (rows, rows, P(), rows)
        + (shard2,) * 4
        + (shard1,) * 4
        + (shard2, shard1, shard1)
        + (shard2,) * 3
        + (owned,) * 3
    )
    outs = (
        (rows, P(), rows)
        + (shard2,) * 4
        + (shard1,) * 4
        + (shard2, shard1, shard1)
        + (shard2,) * 3
        + (owned,) * 3
    )
    return jax.shard_map(
        per_device, mesh=mesh, in_specs=placed, out_specs=outs, check_vma=False
    )
```

```python
import jax
import jax.numpy as jnp
from jax import lax
from jax.experimental import pallas as pl
from jax.experimental.pallas import tpu as pltpu
from jax.sharding import Mesh
from jax.sharding import PartitionSpec as P

HEADS = 16
HD = 128
LANES = 128
PLANES = 4
PAIR = 2
TILE = 256
VMEM_BYTES = 56 * 2**20
ALL = ("z", "x", "y", "c")
GROUP = ("z", "y", "c")

f32 = jnp.float32
bf16 = jnp.bfloat16

epsilon = 1e-06
rope_base = 1000000.0
highest = lax.Precision.HIGHEST
neg_large = -1e30


def mm(left, right, contract=((1,), (0,))):
    return lax.dot_general(left, right, (contract, ((), ())), preferred_element_type=f32)


def mm_t(left, right):
    return mm(left, right, ((1,), (1,)))


def t_mm(left, right):
    return mm(left, right, ((0,), (0,)))


def rope_tables(positions, head_width):
    halfway = head_width // 2
    freqs = rope_base ** (-jnp.arange(halfway, dtype=f32) * 2.0 / head_width)
    angles = positions.astype(f32)[:, None] * freqs[None, :]
    angles = jnp.concatenate([angles, angles], axis=1)
    return (jnp.cos(angles), jnp.sin(angles))


def rotate(values, cosine, sine):
    halfway = values.shape[-1] // 2
    turned = jnp.concatenate([-values[..., halfway:], values[..., :halfway]], axis=-1)
    return values * cosine[:, None, :] + turned * sine[:, None, :]


def rotate_back(grads_in, cosine, sine):
    halfway = grads_in.shape[-1] // 2
    scaled = grads_in * sine[:, None, :]
    turned = jnp.concatenate([scaled[..., halfway:], -scaled[..., :halfway]], axis=-1)
    return grads_in * cosine[:, None, :] + turned


def norm_back(grad_normed, rows_in, inverse, gain):
    weighted = grad_normed * gain
    inner = jnp.sum(weighted * rows_in, axis=-1, keepdims=True)
    grad_rows = inverse * weighted - rows_in * inverse**3 * inner / rows_in.shape[-1]
    grad_gain = jnp.sum(grad_normed * rows_in * inverse, axis=0)
    return (grad_rows, grad_gain)


def add_low(*parts):
    total = parts[0].astype(f32)
    for part in parts[1:]:
        total = total + part.astype(f32)
    return total.astype(bf16)


class Links:
    def __init__(self):
        self.sizes = {axis: lax.axis_size(axis) for axis in ALL}
        self.at = {axis: lax.axis_index(axis) for axis in ALL}
        self.across = self.sizes["x"]
        self.rows = self.sizes["y"]

    def turn(self, value, axis, steps):
        size = self.sizes[axis]
        return lax.ppermute(value, axis, [(i, (i + steps) % size) for i in range(size)])

    def line(self, value, *pairs):
        return lax.ppermute(value, "z", pairs)

    def behind(self, axis, steps):
        return (self.at[axis] - steps) % self.sizes[axis]

    def ahead(self, axis, steps):
        return (self.at[axis] + steps) % self.sizes[axis]

    def planes_held(self):
        return self.behind("z", jnp.arange(PLANES))

    def gather_z(self, value):
        return [value] + [self.turn(value, "z", k) for k in range(1, PLANES)]

    def scatter_z(self, *blocks):
        return [blocks[0]] + [self.turn(blocks[k], "z", -k) for k in range(1, PLANES)]

    def gather_x(self, value):
        return [value] + [self.turn(value, "x", t) for t in range(1, self.across)]

    def exchange_z(self, value):
        return lax.all_to_all(value, "z", split_axis=0, concat_axis=0, tiled=True)

    def place_rows(self, blocks, axis, dim):
        shape = blocks[0].shape[:dim] + (self.sizes[axis],) + blocks[0].shape[dim:]
        buffer = jnp.zeros(shape, blocks[0].dtype)
        for s, block in enumerate(blocks):
            buffer = lax.dynamic_update_slice_in_dim(
                buffer, jnp.expand_dims(block, dim), self.behind(axis, s), dim
            )
        return buffer

    def pick(self, value, index, dim):
        return lax.dynamic_index_in_dim(value, index, dim, keepdims=False)

    def scatter_axis(self, value, axis, dim):
        total = self.pick(value, self.at[axis], dim).astype(f32)
        for s in range(1, self.sizes[axis]):
            total = total + self.turn(
                self.pick(value, self.ahead(axis, s), dim), axis, s
            ).astype(f32)
        return total

    def exchange_group(self, value):
        return lax.all_to_all(value, GROUP, split_axis=0, concat_axis=0, tiled=True)


def after(value, *others):
    return lax.optimization_barrier((value,) + others)[0]


def weight_copies(places_ref, pieces, targets, sems):
    made = []
    across = len(pieces[0])
    for per_weight, target in zip(pieces, targets):
        cols = target.shape[1]
        for t, (source, first) in enumerate(per_weight):
            planes, block = source.shape[:2]
            for z in range(planes):
                row = pl.multiple_of((z * across + places_ref[t]) * block, block)
                view = source.at[z] if first is None else source.at[z, :, pl.ds(first, cols)]
                made.append(
                    pltpu.make_async_copy(
                        view, target.at[pl.ds(row, block)], sems.at[len(made)]
                    )
                )
    return made


def load_weights(places_ref, pieces, targets, sems):
    @pl.when(pl.program_id(0) == 0)
    def _():
        for copy in weight_copies(places_ref, pieces, targets, sems):
            copy.start()
        for copy in weight_copies(places_ref, pieces, targets, sems):
            copy.wait()


def expert_kernel(stacked, carried, across, places_ref, rows_ref, cot_ref, widen_ref, fold_ref, *refs):
    if carried:
        carry_ref, refs = refs[0], refs[1:]
    count = across if stacked else 3 * across
    sources = refs[:count]
    back_ref, hidden_ref, grad_gate_ref, grad_up_ref = refs[count : count + 4]
    gate_w, up_w, down_w, sems = refs[count + 4 :]
    width = cot_ref.shape[1]
    wide = gate_w.shape[1]
    if stacked:
        pieces = [[(source, k * wide) for source in sources] for k in range(3)]
    else:
        pieces = [
            [(source, None) for source in sources[k * across : (k + 1) * across]]
            for k in range(3)
        ]
    load_weights(places_ref, pieces, (gate_w, up_w, down_w), sems)

    payload = rows_ref[...]
    rows = payload[:, :width]
    wide_gate = mm(payload[:, width:], widen_ref[...])
    gate = mm(rows, gate_w[...])
    up = mm(rows, up_w[...])
    grad_hidden = mm(cot_ref[...], down_w[...])
    sigma = 1.0 / (1.0 + jnp.exp(-gate))
    act = gate * sigma
    hidden = act * up
    hidden_ref[...] = (hidden * wide_gate).astype(bf16)
    tail = mm((hidden * grad_hidden).astype(bf16), fold_ref[...])
    grad_hidden = grad_hidden * wide_gate
    grad_gate = (grad_hidden * up * (sigma * (1.0 + gate * (1.0 - sigma)))).astype(bf16)
    grad_up = (grad_hidden * act).astype(bf16)
    grad_gate_ref[...] = grad_gate
    grad_up_ref[...] = grad_up
    back = mm_t(grad_gate, gate_w[...]) + mm_t(grad_up, up_w[...])
    if carried:
        back = back + carry_ref[:, :width].astype(f32)
        tail = tail + carry_ref[:, width:].astype(f32)
    back_ref[:, :width] = back.astype(bf16)
    back_ref[:, width:] = tail.astype(bf16)


def run_experts(places, rows, cot, widen, fold, weights, carry=None):
    stacked = len(weights) == 1
    across = len(weights[0])
    flat = [piece for per_weight in weights for piece in per_weight]
    planes = flat[0].shape[0]
    wide = widen.shape[1]
    count, width = cot.shape
    full = rows.shape[1]
    carries = [] if carry is None else [carry]

    def row_block(cols):
        return pl.BlockSpec((TILE, cols), lambda i, p: (i, 0))

    def whole(a):
        return pl.BlockSpec(a.shape, lambda i, p: (0, 0))

    return pl.pallas_call(
        lambda *refs: expert_kernel(stacked, bool(carries), across, *refs),
        grid_spec=pltpu.PrefetchScalarGridSpec(
            num_scalar_prefetch=1,
            grid=(count // TILE,),
            in_specs=[row_block(full), row_block(width), whole(widen), whole(fold)]
            + [row_block(full)] * len(carries)
            + [pl.BlockSpec(memory_space=pl.ANY)] * len(flat),
            out_specs=[row_block(full)] + [row_block(wide)] * 3,
            scratch_shapes=[pltpu.VMEM((width, wide), bf16)] * 3
            + [pltpu.SemaphoreType.DMA((3 * across * planes,))],
        ),
        out_shape=[jax.ShapeDtypeStruct((count, full), bf16)]
        + [jax.ShapeDtypeStruct((count, wide), bf16)] * 3,
        compiler_params=pltpu.CompilerParams(
            vmem_limit_bytes=VMEM_BYTES, dimension_semantics=("arbitrary",)
        ),
        cost_estimate=pl.CostEstimate(
            flops=2 * count * width * wide * 5,
            bytes_accessed=3 * width * wide * 2 + count * (2 * full + width + 3 * wide) * 2,
            transcendentals=count * wide,
        ),
    )(places, rows, cot, widen, fold, *carries, *flat)


def output_kernel(across, places_ref, order_ref, first_ref, second_ref, *refs):
    firsts, seconds = refs[:across], refs[across : 2 * across]
    out_ref, first_w, second_w, sems = refs[2 * across :]
    extra = second_w.shape[1]
    pieces = [[(r, None) for r in firsts], [(r, 2 * extra) for r in seconds]]
    load_weights(places_ref, pieces, (first_w, second_w), sems)
    out_ref[0] = (mm_t(first_ref[...], first_w[...]) + mm_t(second_ref[...], second_w[...])).astype(bf16)


def run_output(places, order, size, first, second, first_w, second_w):
    across = len(first_w)
    planes, block, cols = first_w[0].shape
    width = planes * across * block
    extra = second.shape[1]
    count = first.shape[0]

    def row_block(a):
        return pl.BlockSpec((size, a.shape[1]), lambda i, p, o: (i, 0))

    return pl.pallas_call(
        lambda *refs: output_kernel(across, *refs),
        grid_spec=pltpu.PrefetchScalarGridSpec(
            num_scalar_prefetch=2,
            grid=(count // size,),
            in_specs=[row_block(first), row_block(second)]
            + [pl.BlockSpec(memory_space=pl.ANY)] * (2 * across),
            out_specs=pl.BlockSpec((1, size, width), lambda i, p, o: (o[i], 0, 0)),
            scratch_shapes=[
                pltpu.VMEM((width, cols), bf16),
                pltpu.VMEM((width, extra), bf16),
                pltpu.SemaphoreType.DMA((2 * across * planes,)),
            ],
        ),
        out_shape=jax.ShapeDtypeStruct((count // size, size, width), bf16),
        compiler_params=pltpu.CompilerParams(
            vmem_limit_bytes=VMEM_BYTES, dimension_semantics=("arbitrary",)
        ),
        cost_estimate=pl.CostEstimate(
            flops=2 * count * width * (cols + extra),
            bytes_accessed=2 * (width + count) * (cols + extra) + 2 * count * width,
            transcendentals=0,
        ),
    )(places, order, first, second, *first_w, *second_w)


def copy_kernel(order_ref, source_ref, target_ref):
    target_ref[...] = source_ref[0]


def take_blocks(blocks, order):
    count, size, width = blocks.shape
    return pl.pallas_call(
        copy_kernel,
        grid_spec=pltpu.PrefetchScalarGridSpec(
            num_scalar_prefetch=1,
            grid=(count,),
            in_specs=[pl.BlockSpec((1, size, width), lambda i, o: (o[i], 0, 0))],
            out_specs=pl.BlockSpec((size, width), lambda i, o: (i, 0)),
        ),
        out_shape=jax.ShapeDtypeStruct((count * size, width), blocks.dtype),
        cost_estimate=pl.CostEstimate(
            flops=0, bytes_accessed=4 * blocks.size, transcendentals=0
        ),
    )(order, blocks)


def term_kernel(groups, *refs):
    out_ref = refs[-1]
    side, block, cols = out_ref.shape[0], out_ref.shape[2], 0
    for pairs in groups:
        total = None
        for left, right in pairs:
            part = t_mm(refs[left][...], refs[right][...])
            total = part if total is None else total + part
        wide = total.shape[1]
        out_ref[:, 0, :, cols : cols + wide] = total.astype(bf16).reshape(side, block, wide)
        cols += wide


def run_terms(groups, width, planes, across):
    block = width // (planes * across)
    side = max(1, LANES // block)
    arrays, numbers = [], []

    def number(a):
        for k, b in enumerate(arrays):
            if a is b:
                return k
        arrays.append(a)
        return len(arrays) - 1

    lefts = set()
    for pairs in groups:
        for left, right in pairs:
            lefts.add(number(left))
    numbers = [[(number(left), number(right)) for left, right in pairs] for pairs in groups]
    wide = sum(pairs[0][1].shape[1] for pairs in groups)
    steps = planes * across // side
    per_plane = across // side

    def spec(k, a):
        if k in lefts:
            return pl.BlockSpec((a.shape[0], side * block), lambda i: (0, i))
        return pl.BlockSpec(a.shape, lambda i: (0, 0))

    flops = sum(2 * l.shape[0] * width * r.shape[1] for pairs in groups for l, r in pairs)
    return pl.pallas_call(
        lambda *refs: term_kernel(numbers, *refs),
        grid=(steps,),
        in_specs=[spec(k, a) for k, a in enumerate(arrays)],
        out_specs=pl.BlockSpec(
            (side, 1, block, wide), lambda i: (i % per_plane, i // per_plane, 0, 0)
        ),
        out_shape=jax.ShapeDtypeStruct((across, planes, block, wide), bf16),
        compiler_params=pltpu.CompilerParams(
            vmem_limit_bytes=VMEM_BYTES, dimension_semantics=("arbitrary",)
        ),
        cost_estimate=pl.CostEstimate(
            flops=flops,
            bytes_accessed=sum(a.size * 2 for a in arrays) + width * wide * 2,
            transcendentals=0,
        ),
    )(*arrays)


def cut_kernel(plans, window, *refs):
    out_ref = refs[-1]
    for k, plan in enumerate(plans):

        @pl.when(pl.program_id(0) == k)
        def _(plan=plan):
            for j, (source, lead, start) in enumerate(plan):
                ref = refs[source]
                cols = slice(start, start + window)
                block = ref[:, cols] if lead is None else ref[lead, :, cols]
                out_ref[0, :, j * window : (j + 1) * window] = block


def cut_columns(arrays, plans, window):
    rows = arrays[0].shape[-2]
    wide = len(plans[0]) * window

    def whole(a):
        return pl.BlockSpec(a.shape, lambda i, n=a.ndim: (0,) * n)

    return pl.pallas_call(
        lambda *refs: cut_kernel(plans, window, *refs),
        grid=(len(plans),),
        in_specs=[whole(a) for a in arrays],
        out_specs=pl.BlockSpec((1, rows, wide), lambda i: (i, 0, 0)),
        out_shape=jax.ShapeDtypeStruct((len(plans), rows, wide), bf16),
        compiler_params=pltpu.CompilerParams(dimension_semantics=("arbitrary",)),
        cost_estimate=pl.CostEstimate(
            flops=0,
            bytes_accessed=2 * (sum(a.size for a in arrays) + len(plans) * rows * wide),
            transcendentals=0,
        ),
    )(*arrays)


def per_device(
    tokens,
    cotangent,
    lengths,
    routes,
    query_weight,
    key_weight,
    value_weight,
    output_weight,
    query_bias,
    key_bias,
    value_bias,
    attention_gain,
    router_weight,
    shared_switch,
    mixer_gain,
    shared_gate_weight,
    shared_up_weight,
    shared_down_weight,
    expert_gate,
    expert_up,
    expert_down,
):
    net = Links()
    across, yrows = net.across, net.rows
    dp_size = PLANES * across
    groups = yrows * PAIR
    rows = tokens.shape[1]
    width = tokens.shape[2]
    top_count = routes.shape[2]
    local_experts = expert_gate.shape[0]
    num_experts = local_experts * groups
    units = local_experts + 1
    inner = expert_gate.shape[2]
    weight_rows = expert_gate.shape[1]
    shard = query_weight.shape[0]
    head_cols = width // PLANES
    heads = head_cols // HD
    window = -(-inner // (PLANES * LANES)) * LANES
    scale = HD ** (-0.5)
    all_slots = float(groups * rows * dp_size)
    iz, ix, iy, ic = net.at["z"], net.at["x"], net.at["y"], net.at["c"]
    expert_at = iy * PAIR + ic

    tok = tokens.reshape(rows, width)
    cot = cotangent.reshape(rows, width)
    length = jnp.take(lengths, expert_at)
    own_start = (iz * across + ix) * rows
    positions = own_start + jnp.arange(rows)
    valid = positions < length
    live = valid.astype(f32)[:, None]
    token_rows = tok.astype(f32)
    grad_final = cot.astype(f32) * live

    tok_blocks = net.gather_z(tok)
    extras = jnp.concatenate(
        [
            attention_gain[:, None],
            mixer_gain[:, None],
            shared_switch[:, None],
            router_weight,
            jnp.zeros((shard, LANES - 3 - num_experts), bf16),
        ],
        axis=1,
    )

    def by_plane(w):
        return jnp.transpose(w.reshape(shard, PLANES, head_cols), (1, 0, 2))

    qkv_own = jnp.concatenate(
        [by_plane(w) for w in (query_weight, key_weight, value_weight)]
        + [jnp.broadcast_to(extras[None], (PLANES, shard, LANES))],
        axis=2,
    )
    qkv_own = net.exchange_z(qkv_own)
    starts = [min(k * window, inner - window) for k in range(PLANES)]
    plans = [[(0, j, s) for j in range(local_experts)] for s in starts]
    down_cut, gate_cut, up_cut = [
        cut_columns([w], plans, window) for w in (expert_down, expert_gate, expert_up)
    ]
    shared_cut = cut_columns(
        [shared_gate_weight, shared_up_weight, shared_down_weight],
        [
            [(k, None, e * inner + s) for k in range(3)]
            for s in starts
            for e in range(groups)
        ],
        window,
    )
    cot_all = lax.all_gather(cot, GROUP)
    down_own = net.exchange_z(after(down_cut, qkv_own))
    if across == 2 and yrows == 2:
        half = PLANES // 2
        from_x = net.turn(qkv_own, "x", 1)
        from_y = net.turn(qkv_own, "y", 1)
        across_both = jnp.concatenate(
            [net.turn(from_y[:half], "x", 1), net.turn(from_x[half:], "y", 1)], axis=0
        )
        across_both = after(across_both, down_own)
        qkv_w = net.place_rows(
            [
                net.place_rows([qkv_own, from_x], "x", 1),
                net.place_rows([from_y, across_both], "x", 1),
            ],
            "y",
            2,
        )
    else:
        qkv_w = net.place_rows(net.gather_x(qkv_own), "x", 1)
        qkv_w = net.place_rows([net.turn(qkv_w, "y", t) if t else qkv_w for t in range(yrows)], "y", 2)
    gate_own = net.exchange_z(after(gate_cut, qkv_w))
    qkv_w = net.place_rows([qkv_w, net.turn(qkv_w, "c", 1)], "c", 3)
    qkv_w = qkv_w.reshape(width, 3 * head_cols + LANES)
    small = qkv_w[:, 3 * head_cols :]
    qkv_w = qkv_w[:, : 3 * head_cols]
    small_rows = mm_t(jnp.eye(16, LANES, dtype=bf16), small)
    attn_gain_f = small_rows[0]
    mixer_gain_f = small_rows[1]
    switch_full = small[:, 2]
    switch_row = small_rows[2]
    router_full = small[:, 3 : 3 + num_experts]

    biases = jnp.concatenate(
        [
            query_bias[:, None],
            key_bias[:, None],
            value_bias[:, None],
            jnp.zeros((shard, LANES - 3), bf16),
        ],
        axis=1,
    )
    out_w = jnp.concatenate([output_weight, biases], axis=1)
    out_w = net.place_rows(net.gather_x(out_w), "x", 0)
    out_w = net.place_rows([out_w, net.turn(out_w, "y", 1)], "y", 1)
    out_w = net.place_rows([out_w, net.turn(out_w, "c", 1)], "c", 2)
    out_w = out_w.reshape(head_cols, width + LANES)
    bias_cols = out_w[:, width : width + 3].astype(f32)
    out_w = out_w[:, :width]
    qkv_bias = jnp.concatenate([bias_cols[:, 0], bias_cols[:, 1], bias_cols[:, 2]])

    def gather_rows(blocks):
        pairs = [
            jnp.concatenate(
                [
                    b if t == 0 else net.turn(b, "y", t)
                    for b in blocks[k : k + 2]
                    for t in range(yrows)
                ],
                axis=0,
            )
            for k in (0, 2)
        ]
        return jnp.concatenate(pairs + [net.turn(pair, "c", 1) for pair in pairs], axis=0)

    def row_sum(pair):
        total = pair[:, 0]
        for t in range(1, yrows):
            total = add_low(total, net.turn(pair[:, t], "y", -t))
        return total

    block_c = jnp.arange(PAIR)[:, None, None]
    block_z = jnp.arange(PLANES)[None, :, None]
    block_y = jnp.arange(yrows)[None, None, :]
    block_order = (
        (net.behind("z", block_z) * yrows + net.behind("y", block_y)) * PAIR
        + net.behind("c", block_c)
    ).reshape(-1)
    block_order = block_order.astype(jnp.int32)
    places = net.behind("x", jnp.arange(across)).astype(jnp.int32)

    hidden_rows = jnp.concatenate(tok_blocks, axis=0)
    hidden_f = hidden_rows.astype(f32)
    attn_inv_group = lax.rsqrt(jnp.mean(hidden_f * hidden_f, axis=-1, keepdims=True) + epsilon)
    normed_attn = (hidden_f * attn_inv_group * attn_gain_f).astype(bf16)
    qkv_pre = mm(normed_attn, qkv_w) + qkv_bias
    planes_held = net.planes_held()
    query_pos = jnp.concatenate(
        [
            (planes_held[s] * across + ix) * rows + jnp.arange(rows)
            for s in range(PLANES)
        ]
    )
    group_rows = PLANES * rows
    cosine, sine = rope_tables(query_pos, HD)
    queries = rotate(
        qkv_pre[:, :head_cols].reshape(group_rows, heads, HD), cosine, sine
    ).astype(bf16)
    keys_own = (
        rotate(
            qkv_pre[:, head_cols : 2 * head_cols].reshape(group_rows, heads, HD), cosine, sine
        )
        .astype(bf16)
        .reshape(group_rows, head_cols)
    )
    values_own = qkv_pre[:, 2 * head_cols :].astype(bf16)
    keys_values = net.gather_x(jnp.concatenate([keys_own, values_own], axis=1))
    key_pos = jnp.concatenate(
        [query_pos + (net.behind("x", t) - ix) * rows for t in range(across)]
    )
    all_kv = after(jnp.concatenate(keys_values, axis=0), gate_own)
    up_own = net.exchange_z(after(up_cut, all_kv))
    cot_group = take_blocks(cot_all.reshape(-1, rows, width), block_order)
    keys_all = all_kv[:, :head_cols].reshape(-1, heads, HD)
    values_all = all_kv[:, head_cols:].reshape(-1, heads, HD)
    scores = jnp.einsum("qhd,khd->hqk", queries, keys_all, preferred_element_type=f32) * scale
    allowed = (key_pos[None, :] <= query_pos[:, None]) & (key_pos[None, :] < length)
    scores = jnp.where(allowed[None], scores, neg_large)
    attn_weights = jax.nn.softmax(scores, axis=-1)
    weights_low = attn_weights.astype(bf16)
    mixed = jnp.einsum("hqk,khd->qhd", weights_low, values_all, preferred_element_type=f32)
    mixed = mixed.astype(bf16).reshape(group_rows, head_cols)
    down_pieces = net.gather_x(down_own)
    mixed = after(mixed, *down_pieces)
    branch = mm(mixed, out_w).astype(bf16).reshape(PLANES, rows, width)
    resid = token_rows
    for part in net.scatter_z(*[branch[s] for s in range(PLANES)]):
        resid = resid + part.astype(f32)

    mix_inv = lax.rsqrt(jnp.mean(resid * resid, axis=-1, keepdims=True) + epsilon)
    normed_mix = (resid * mix_inv * mixer_gain_f).astype(bf16)
    logits = mm(normed_mix, router_full)
    probs = jax.nn.softmax(logits, axis=-1)
    route_ids = routes.reshape(rows, top_count)
    chosen = (route_ids[:, :, None] == jnp.arange(num_experts)[None, None, :]) & valid[
        :, None, None
    ]
    chosen_any = jnp.sum(chosen.astype(f32), axis=1)
    gates = probs * chosen_any
    switch = jax.nn.sigmoid(mm(normed_mix, switch_full[:, None]))
    gate_count = num_experts + 1

    def two_parts(value):
        high = lax.reduce_precision(value, 8, 7)
        return [high.astype(bf16), (value - high).astype(bf16)]

    parts = two_parts(jnp.concatenate([gates, switch * live], axis=1))
    parts += [chosen_any.astype(bf16)] + two_parts(probs * live)
    extra_at = 2 * gate_count
    extra_count = 3 * num_experts
    parts.append(jnp.zeros((rows, LANES - extra_at - extra_count), bf16))
    mix_blocks = net.gather_z(jnp.concatenate([normed_mix] + parts, axis=1))
    mix_blocks = [after(b, up_own) for b in mix_blocks]
    shared_own = net.exchange_group(after(shared_cut, *mix_blocks))
    shared_own = shared_own.reshape(PLANES, weight_rows, 3 * window)
    weight_parts = [net.gather_x(gate_own), net.gather_x(up_own), down_pieces]
    shared_parts = [net.gather_x(shared_own)]
    mix_group = gather_rows(mix_blocks)

    block_sums = jnp.sum(
        mix_group[:, width + extra_at : width + extra_at + extra_count]
        .astype(f32)
        .reshape(PAIR * PLANES * yrows, rows, extra_count),
        axis=1,
    )
    block_sums = jnp.zeros_like(block_sums).at[block_order].set(block_sums)
    sums = jnp.sum(block_sums.reshape(-1, extra_count), axis=0, keepdims=True)
    sums = jnp.sum(net.place_rows(net.gather_x(sums), "x", 0)[:, 0], axis=0)
    count_all = sums[:num_experts]
    mass_all = sums[num_experts : 2 * num_experts] + sums[2 * num_experts :]
    fraction = count_all / (top_count * all_slots)
    balance_loss = (num_experts * jnp.sum(fraction * mass_all / all_slots)).reshape(1)

    column = jnp.arange(window)
    fresh = column + jnp.minimum(iz * window, inner - window) >= iz * window
    unit_at = jnp.concatenate(
        [
            expert_at * local_experts + jnp.arange(local_experts),
            jnp.full((1,), num_experts),
        ]
    )
    unit_at = jnp.broadcast_to(unit_at[:, None], (units, window)).reshape(-1)
    fresh = jnp.tile(fresh, units)
    lane = jnp.arange(LANES)
    lane_gate = jnp.where(lane < extra_at, lane % gate_count, -1)
    widen = ((lane_gate[:, None] == unit_at[None]) & fresh[None]).astype(bf16)
    fold = ((lane[None] == unit_at[:, None]) & fresh[:, None]).astype(bf16)
    split = local_experts * window
    routed = run_experts(
        places, mix_group, cot_group, widen[:, :split], fold[:split], weight_parts
    )
    shared = run_experts(
        places, mix_group, cot_group, widen[:, split:], fold[split:], shared_parts, routed[0]
    )
    back = shared[0].reshape(PAIR, PLANES, yrows, rows, -1)
    pair = add_low(back[0], net.turn(back[1], "c", 1))
    kept_far = row_sum(pair[1:3])
    kept_near = row_sum(jnp.stack([pair[0], pair[3]]))

    shared_term = run_terms(
        [
            [(after(mix_group, pair), shared[2])],
            [(after(mix_group, pair), shared[3])],
            [(after(cot_group, pair), shared[1])],
        ],
        width,
        PLANES,
        across,
    )
    mix_late = after(mix_group, shared_term, kept_far)
    pair_term = run_terms(
        [[(mix_late, routed[2])], [(mix_late, routed[3])]], width, PLANES, across
    )
    down_term = run_terms(
        [[(after(cot_group, pair_term, kept_near), routed[1])]], width, PLANES, across
    )
    grad_sum = sum(
        part.astype(f32)
        for part in net.scatter_z(kept_near[0], kept_far[0], kept_far[1], kept_near[1])
    )
    grad_sum = after(grad_sum, down_term)
    scattered = [
        net.scatter_axis(term, "x", 0).astype(bf16)
        for term in (shared_term, pair_term, down_term)
    ]
    grad_gates = grad_sum[:, width : width + num_experts]
    grad_switch = grad_sum[:, width + num_experts : width + gate_count]
    grad_switch_logit = grad_switch * live * switch * (1.0 - switch)
    grad_probs = grad_gates * chosen_any * live + live * (num_experts * fraction / all_slots)[None, :]
    grad_logits = (
        probs * (grad_probs - jnp.sum(probs * grad_probs, axis=1, keepdims=True))
    ).astype(bf16)
    grad_normed_mix = (
        grad_sum[:, :width]
        + grad_switch_logit * switch_row[None, :]
        + mm_t(grad_logits, router_full)
    )
    grad_mix_rows, grad_mixer_gain = norm_back(grad_normed_mix, resid, mix_inv, mixer_gain_f)
    grad_resid = grad_final + grad_mix_rows
    grad_branch = grad_resid.astype(bf16)
    branch_group = jnp.concatenate(net.gather_z(grad_branch), axis=0)
    out_blocks = run_output(
        places,
        block_order,
        rows,
        after(routed[1], grad_branch),
        shared[1],
        down_pieces,
        shared_parts[0],
    )
    branch_group = after(branch_group, out_blocks)
    out_sum = lax.psum_scatter(out_blocks, GROUP, scatter_dimension=0, tiled=True)[0]
    sorted_grads = [net.exchange_group(after(scattered[0], branch_group).reshape(-1, shard, 3 * window))]
    for part in scattered[1:]:
        sorted_grads.append(net.exchange_z(after(part, sorted_grads[-1])))

    grad_mixed = mm_t(branch_group, out_w).astype(bf16).reshape(group_rows, heads, HD)
    grad_attn = jnp.einsum("qhd,khd->hqk", grad_mixed, values_all, preferred_element_type=f32)
    delta = jnp.sum(attn_weights * grad_attn, axis=-1, keepdims=True)
    grad_scores = (attn_weights * (grad_attn - delta)).astype(bf16)
    grad_keys = (
        jnp.einsum("hqk,qhd->khd", grad_scores, queries, preferred_element_type=f32) * scale
    )
    grad_values = jnp.einsum("hqk,qhd->khd", weights_low, grad_mixed, preferred_element_type=f32)
    grad_kv = jnp.concatenate(
        [grad_keys.reshape(-1, head_cols), grad_values.reshape(-1, head_cols)], axis=1
    ).reshape(across, group_rows, 2 * head_cols)
    grad_kv_own = grad_kv[0]
    for t in range(1, across):
        grad_kv_own = grad_kv_own + net.turn(grad_kv[t].astype(bf16), "x", -t).astype(f32)
    grad_queries = (
        jnp.einsum("hqk,khd->qhd", grad_scores, keys_all, preferred_element_type=f32) * scale
    )
    grad_query_pre = (
        rotate_back(grad_queries, cosine, sine).reshape(group_rows, head_cols).astype(bf16)
    )
    grad_key_pre = (
        rotate_back(grad_kv_own[:, :head_cols].reshape(group_rows, heads, HD), cosine, sine)
        .reshape(group_rows, head_cols)
        .astype(bf16)
    )
    grad_value_pre = grad_kv_own[:, head_cols:].astype(bf16)
    grad_qkv = jnp.concatenate([grad_query_pre, grad_key_pre, grad_value_pre], axis=1)
    grad_qkv = after(grad_qkv, sorted_grads[0])
    grad_normed_part = mm_t(grad_qkv, qkv_w)
    gain_part = jnp.sum(grad_normed_part * hidden_f * attn_inv_group, axis=0)
    normed_part_low = grad_normed_part.astype(bf16).reshape(PLANES, rows, width)
    grad_normed_attn = jnp.zeros((rows, width), f32)
    for part in net.scatter_z(*[normed_part_low[s] for s in range(PLANES)]):
        grad_normed_attn = grad_normed_attn + part.astype(f32)
    attn_inv = attn_inv_group[:rows]
    grad_attn_rows, _ = norm_back(grad_normed_attn, token_rows, attn_inv, attn_gain_f)
    grad_tokens = (grad_resid + grad_attn_rows).astype(bf16).reshape(1, rows, width)

    layer_out = ((resid + out_sum.astype(f32)) * live).astype(bf16)

    def unit_columns(by_plane, j):
        cols = [by_plane[k, :, j * window : (j + 1) * window] for k in range(PLANES)]
        used = window * (PLANES - 1)
        cols[-1] = cols[-1][:, window - (inner - used) :]
        return jnp.concatenate(cols, axis=1)

    def routed_grads(by_plane):
        return jnp.stack(
            [unit_columns(by_plane, j) for j in range(local_experts)]
        ).astype(f32)

    grad_expert_gate = routed_grads(sorted_grads[1][:, :, :split])
    grad_expert_up = routed_grads(sorted_grads[1][:, :, split:])
    grad_expert_down = routed_grads(sorted_grads[2])
    shared_back = sorted_grads[0].reshape(PLANES, groups, shard, 3 * window)
    shared_grads = []
    for k in range(3):
        cols = []
        for e in range(groups):
            for z in range(PLANES):
                first = k * window + (window * PLANES - inner if z == PLANES - 1 else 0)
                cols.append(shared_back[z, e, :, first : (k + 1) * window])
        shared_grads.append(jnp.concatenate(cols, axis=1).astype(f32))

    def to_rows(part, dims):
        part = net.scatter_axis(part, "c", dims - 1).astype(bf16)
        cut = part.shape[-1] // (2 * LANES) * LANES
        if across > 2:
            cut = part.shape[-1]
        first = net.scatter_axis(part[..., :cut], "y", dims - 2).astype(bf16)
        first = net.scatter_axis(first, "x", dims - 3).astype(bf16)
        if cut == part.shape[-1]:
            return first
        second = net.scatter_axis(part[..., cut:], "x", dims - 3).astype(bf16)
        second = net.scatter_axis(second, "y", dims - 3).astype(bf16)
        return jnp.concatenate([first, second], axis=-1)

    grad_out_w = t_mm(mixed, branch_group).astype(bf16)
    grad_output_weight = to_rows(
        grad_out_w.reshape(across, yrows, PAIR, shard, width), 3
    ).astype(f32)
    row_terms = jnp.concatenate(
        [
            t_mm(grad_logits, normed_mix),
            jnp.sum(grad_switch_logit * normed_mix.astype(f32), axis=0)[None],
            grad_mixer_gain[None],
            gain_part[None],
            jnp.zeros((16 - num_experts - 3, width), f32),
        ],
        axis=0,
    ).astype(bf16)
    qkv_term = run_terms(
        [[(normed_attn, grad_qkv)], [(row_terms, jnp.eye(16, LANES, dtype=bf16))]],
        width,
        PLANES,
        across,
    )
    qkv_rows = to_rows(
        jnp.swapaxes(qkv_term.reshape(across, PLANES, yrows, PAIR, shard, -1), 0, 1), 4
    )
    qkv_planes = net.exchange_z(qkv_rows)
    grad_qkv_weights = [
        jnp.concatenate(
            [qkv_planes[k, :, j * head_cols : (j + 1) * head_cols] for k in range(PLANES)], axis=1
        ).astype(f32)
        for j in range(3)
    ]

    row_grads = jnp.sum(
        qkv_planes[:, :, 3 * head_cols : 3 * head_cols + num_experts + 3].astype(f32), axis=0
    )

    bias_part = jnp.sum(grad_qkv.astype(f32), axis=0).reshape(3, across, yrows, PAIR, shard)
    bias_part = jnp.transpose(bias_part, (1, 2, 3, 0, 4))
    bias_part = net.scatter_axis(bias_part, "c", 2)
    bias_part = net.scatter_axis(bias_part, "y", 1)
    bias_part = net.scatter_axis(bias_part, "x", 0)
    return (
        layer_out.reshape(1, rows, width),
        balance_loss,
        grad_tokens,
        grad_qkv_weights[0],
        grad_qkv_weights[1],
        grad_qkv_weights[2],
        grad_output_weight,
        bias_part[0],
        bias_part[1],
        bias_part[2],
        row_grads[:, num_experts + 2],
        row_grads[:, :num_experts],
        row_grads[:, num_experts],
        row_grads[:, num_experts + 1],
        shared_grads[0],
        shared_grads[1],
        shared_grads[2],
        grad_expert_gate,
        grad_expert_up,
        grad_expert_down,
    )


def solution(mesh):
    dp_size, expert_size = mesh.devices.shape
    shape = (PLANES, dp_size // PLANES, expert_size // PAIR, PAIR)
    fine = Mesh(mesh.devices.reshape(shape), ALL)
    rows = P(("y", "c"), ("z", "x"), None)
    shard2 = P(ALL, None)
    shard1 = P(ALL)
    placed = (
        (rows, rows, P(), rows)
        + (shard2,) * 4
        + (shard1,) * 4
        + (shard2, shard1, shard1)
        + (shard2,) * 3
        + (rows,) * 3
    )
    outs = (
        (rows, P(), rows)
        + (shard2,) * 4
        + (shard1,) * 4
        + (shard2, shard1, shard1)
        + (shard2,) * 3
        + (rows,) * 3
    )
    return jax.shard_map(
        per_device, mesh=fine, in_specs=placed, out_specs=outs, check_vma=False
    )
```

```python
import jax
import jax.numpy as jnp
from jax import lax
from jax.experimental import pallas as pl
from jax.experimental.pallas import tpu as pltpu
from jax.sharding import Mesh
from jax.sharding import PartitionSpec as P

HEADS = 16
HD = 128
LANES = 128
PLANES = 4
PAIR = 2
VMEM_BYTES = 56 * 2**20
ALL = ("z", "x", "y", "c")
GROUP = ("z", "y", "c")
TILES = ("c", "z", "y")

f32 = jnp.float32
bf16 = jnp.bfloat16

epsilon = 1e-06
rope_base = 1000000.0
highest = lax.Precision.HIGHEST
neg_large = -1e30


def mm(left, right, contract=((1,), (0,))):
    return lax.dot_general(left, right, (contract, ((), ())), preferred_element_type=f32)


def mm_t(left, right):
    return mm(left, right, ((1,), (1,)))


def t_mm(left, right):
    return mm(left, right, ((0,), (0,)))


def rope_tables(positions, head_width):
    halfway = head_width // 2
    freqs = rope_base ** (-jnp.arange(halfway, dtype=f32) * 2.0 / head_width)
    angles = positions.astype(f32)[:, None] * freqs[None, :]
    angles = jnp.concatenate([angles, angles], axis=1)
    return (jnp.cos(angles), jnp.sin(angles))


def rotate(values, cosine, sine):
    halfway = values.shape[-1] // 2
    turned = jnp.concatenate([-values[..., halfway:], values[..., :halfway]], axis=-1)
    return values * cosine[:, None, :] + turned * sine[:, None, :]


def rotate_back(grads_in, cosine, sine):
    halfway = grads_in.shape[-1] // 2
    scaled = grads_in * sine[:, None, :]
    turned = jnp.concatenate([scaled[..., halfway:], -scaled[..., :halfway]], axis=-1)
    return grads_in * cosine[:, None, :] + turned


def norm_back(grad_normed, rows_in, inverse, gain):
    weighted = grad_normed * gain
    inner = jnp.sum(weighted * rows_in, axis=-1, keepdims=True)
    grad_rows = inverse * weighted - rows_in * inverse**3 * inner / rows_in.shape[-1]
    grad_gain = jnp.sum(grad_normed * rows_in * inverse, axis=0)
    return (grad_rows, grad_gain)


def add_low(*parts):
    total = parts[0].astype(f32)
    for part in parts[1:]:
        total = total + part.astype(f32)
    return total.astype(bf16)


class Links:
    def __init__(self):
        self.sizes = {axis: lax.axis_size(axis) for axis in ALL}
        self.at = {axis: lax.axis_index(axis) for axis in ALL}
        self.across = self.sizes["x"]
        self.rows = self.sizes["y"]

    def turn(self, value, axis, steps):
        size = self.sizes[axis]
        return lax.ppermute(value, axis, [(i, (i + steps) % size) for i in range(size)])

    def line(self, value, *pairs):
        return lax.ppermute(value, "z", pairs)

    def behind(self, axis, steps):
        return (self.at[axis] - steps) % self.sizes[axis]

    def ahead(self, axis, steps):
        return (self.at[axis] + steps) % self.sizes[axis]

    def planes_held(self):
        return self.behind("z", jnp.arange(PLANES))

    def gather_z(self, value):
        return [value] + [self.turn(value, "z", k) for k in range(1, PLANES)]

    def scatter_z(self, *blocks):
        return [blocks[0]] + [self.turn(blocks[k], "z", -k) for k in range(1, PLANES)]

    def gather_x(self, value):
        return [value] + [self.turn(value, "x", t) for t in range(1, self.across)]

    def exchange_z(self, value):
        return lax.all_to_all(value, "z", split_axis=0, concat_axis=0, tiled=True)

    def place_rows(self, blocks, axis, dim):
        shape = blocks[0].shape[:dim] + (self.sizes[axis],) + blocks[0].shape[dim:]
        buffer = jnp.zeros(shape, blocks[0].dtype)
        for s, block in enumerate(blocks):
            buffer = lax.dynamic_update_slice_in_dim(
                buffer, jnp.expand_dims(block, dim), self.behind(axis, s), dim
            )
        return buffer

    def pick(self, value, index, dim):
        return lax.dynamic_index_in_dim(value, index, dim, keepdims=False)

    def scatter_axis(self, value, axis, dim):
        total = self.pick(value, self.at[axis], dim).astype(f32)
        for s in range(1, self.sizes[axis]):
            total = total + self.turn(
                self.pick(value, self.ahead(axis, s), dim), axis, s
            ).astype(f32)
        return total

    def exchange_group(self, value):
        return lax.all_to_all(value, GROUP, split_axis=0, concat_axis=0, tiled=True)


def after(value, *others):
    return lax.optimization_barrier((value,) + others)[0]


def weight_copies(places_ref, pieces, targets, sems):
    made = []
    across = len(pieces[0])
    for per_weight, target in zip(pieces, targets):
        cols = target.shape[1]
        for t, (source, first) in enumerate(per_weight):
            planes, block = source.shape[:2]
            for z in range(planes):
                row = pl.multiple_of((z * across + places_ref[t]) * block, block)
                view = source.at[z, :, pl.ds(first, cols)]
                made.append(
                    pltpu.make_async_copy(
                        view, target.at[pl.ds(row, block)], sems.at[len(made)]
                    )
                )
    return made


def load_weights(places_ref, pieces, targets, sems):
    @pl.when(pl.program_id(0) == 0)
    def _():
        for copy in weight_copies(places_ref, pieces, targets, sems):
            copy.start()
        for copy in weight_copies(places_ref, pieces, targets, sems):
            copy.wait()


def expert_kernel(second, across, places_ref, order_ref, rows_ref, cot_ref, widen_ref, fold_ref, *refs):
    tile = rows_ref.shape[0]
    half = tile // 2
    own_at = pl.multiple_of(places_ref[across] * half, half)
    other_at = pl.multiple_of(half - own_at, half)
    if second:
        carry_ref, first_ref, refs = refs[0], refs[1], refs[2:]
    count = 2 * across if second else across
    outs, scratch = refs[count : count + 5], refs[count + 5 :]
    wide = scratch[0].shape[1]
    pieces = [[(source, k * wide) for source in refs[:across]] for k in range(3)]
    if second:
        pieces.append([(source, 2 * first_ref.shape[1]) for source in refs[across:count]])
    back_ref, hidden_ref, grad_gate_ref, grad_up_ref, last_ref = outs
    gate_w, up_w, down_w = scratch[:3]
    load_weights(places_ref, pieces, scratch[:-1], scratch[-1])
    if second:
        cot = cot_ref[...]
    else:
        cot = jnp.concatenate(
            [cot_ref[0, pl.ds(own_at, half)], cot_ref[0, pl.ds(other_at, half)]], axis=0
        )
        last_ref[...] = cot
    width = cot.shape[1]
    payload = rows_ref[...]
    rows = payload[:, :width]
    wide_gate = mm(payload[:, width:], widen_ref[...])
    gate = mm(rows, gate_w[...])
    up = mm(rows, up_w[...])
    grad_hidden = mm(cot, down_w[...])
    sigma = 1.0 / (1.0 + jnp.exp(-gate))
    act = gate * sigma
    hidden = act * up
    hidden_gated = (hidden * wide_gate).astype(bf16)
    hidden_ref[...] = hidden_gated
    tail = mm((hidden * grad_hidden).astype(bf16), fold_ref[...])
    grad_hidden = grad_hidden * wide_gate
    grad_gate = (grad_hidden * up * (sigma * (1.0 + gate * (1.0 - sigma)))).astype(bf16)
    grad_up = (grad_hidden * act).astype(bf16)
    grad_gate_ref[...] = grad_gate
    grad_up_ref[...] = grad_up
    back = mm_t(grad_gate, gate_w[...]) + mm_t(grad_up, up_w[...])
    if second:
        back = back + carry_ref[:, :width].astype(f32)
        tail = tail + carry_ref[:, width:].astype(f32)
        out = mm_t(first_ref[...], scratch[3][...]) + mm_t(hidden_gated, down_w[...])
        last_ref[0, pl.ds(own_at, half)] = out[:half].astype(bf16)
        last_ref[0, pl.ds(other_at, half)] = out[half:].astype(bf16)
    back_ref[:, :width] = back.astype(bf16)
    back_ref[:, width:] = tail.astype(bf16)


def run_experts(places, order, tile, rows, cot, widen, fold, weights, carry=None, first=None):
    second = carry is not None
    across = len(weights[0])
    flat = [piece for per_weight in weights for piece in per_weight]
    planes = flat[0].shape[0]
    wide = widen.shape[1]
    count, full = rows.shape
    width = cot.shape[-1]

    def row_block(cols):
        return pl.BlockSpec((tile, cols), lambda i, p, o: (i, 0))

    def whole(a):
        return pl.BlockSpec(a.shape, lambda i, p, o: (0, 0))

    placed = pl.BlockSpec((1, tile, width), lambda i, p, o: (o[i], 0, 0))
    extra = [carry, first] if second else []
    scratch = [pltpu.VMEM((width, wide), bf16)] * 3
    if second:
        scratch.append(pltpu.VMEM((width, first.shape[1]), bf16))
    return pl.pallas_call(
        lambda *refs: expert_kernel(second, across, *refs),
        grid_spec=pltpu.PrefetchScalarGridSpec(
            num_scalar_prefetch=2,
            grid=(count // tile,),
            in_specs=[
                row_block(full),
                row_block(width) if second else placed,
                whole(widen),
                whole(fold),
            ]
            + [row_block(a.shape[1]) for a in extra]
            + [pl.BlockSpec(memory_space=pl.ANY)] * len(flat),
            out_specs=[row_block(full)]
            + [row_block(wide)] * 3
            + [placed if second else row_block(width)],
            scratch_shapes=scratch
            + [pltpu.SemaphoreType.DMA((len(scratch) * across * planes,))],
        ),
        out_shape=[jax.ShapeDtypeStruct((count, full), bf16)]
        + [jax.ShapeDtypeStruct((count, wide), bf16)] * 3
        + [
            jax.ShapeDtypeStruct(
                (count // tile, tile, width) if second else (count, width), bf16
            )
        ],
        compiler_params=pltpu.CompilerParams(
            vmem_limit_bytes=VMEM_BYTES, dimension_semantics=("arbitrary",)
        ),
        cost_estimate=pl.CostEstimate(
            flops=2 * count * width * wide * 5,
            bytes_accessed=3 * width * wide * 2 + count * (3 * full + 2 * width + 3 * wide) * 2,
            transcendentals=count * wide,
        ),
    )(places, order, rows, cot, widen, fold, *extra, *flat)


def term_kernel(sets, *refs):
    out_refs = refs[len(refs) - len(sets) :]
    for groups, out_ref in zip(sets, out_refs):
        side, block, cols = out_ref.shape[0], out_ref.shape[2], 0
        for left, right in groups:
            part = t_mm(refs[left][...], refs[right][...])
            wide = part.shape[1]
            out_ref[:, 0, :, cols : cols + wide] = part.astype(bf16).reshape(side, block, wide)
            cols += wide


def run_terms(sets, width, planes, across):
    block = width // (planes * across)
    side = max(1, LANES // block)
    arrays, lefts = [], set()

    def number(a):
        for k, b in enumerate(arrays):
            if a is b:
                return k
        arrays.append(a)
        return len(arrays) - 1

    numbers = [[(number(left), number(right)) for left, right in pairs] for pairs in sets]
    for pairs in numbers:
        lefts.update(left for left, _ in pairs)
    wides = [sum(right.shape[1] for _, right in pairs) for pairs in sets]
    per_plane = across // side

    def spec(k, a):
        if k in lefts:
            return pl.BlockSpec((a.shape[0], side * block), lambda i: (0, i))
        return pl.BlockSpec(a.shape, lambda i: (0, 0))

    flops = sum(2 * l.shape[0] * width * r.shape[1] for pairs in sets for l, r in pairs)
    return pl.pallas_call(
        lambda *refs: term_kernel(numbers, *refs),
        grid=(planes * across // side,),
        in_specs=[spec(k, a) for k, a in enumerate(arrays)],
        out_specs=[
            pl.BlockSpec((side, 1, block, wide), lambda i: (i % per_plane, i // per_plane, 0, 0))
            for wide in wides
        ],
        out_shape=[jax.ShapeDtypeStruct((across, planes, block, wide), bf16) for wide in wides],
        compiler_params=pltpu.CompilerParams(
            vmem_limit_bytes=VMEM_BYTES, dimension_semantics=("arbitrary",)
        ),
        cost_estimate=pl.CostEstimate(
            flops=flops,
            bytes_accessed=sum(a.size * 2 for a in arrays) + width * sum(wides) * 2,
            transcendentals=0,
        ),
    )(*arrays)


def cut_kernel(plans, window, *refs):
    out_ref = refs[-1]
    for k, plan in enumerate(plans):

        @pl.when(pl.program_id(0) == k)
        def _(plan=plan):
            for j, (source, lead, start) in enumerate(plan):
                ref = refs[source]
                cols = slice(start, start + window)
                block = ref[:, cols] if lead is None else ref[lead, :, cols]
                out_ref[0, :, j * window : (j + 1) * window] = block


def cut_columns(arrays, plans, window):
    rows = arrays[0].shape[-2]
    wide = len(plans[0]) * window

    def whole(a):
        return pl.BlockSpec(a.shape, lambda i, n=a.ndim: (0,) * n)

    return pl.pallas_call(
        lambda *refs: cut_kernel(plans, window, *refs),
        grid=(len(plans),),
        in_specs=[whole(a) for a in arrays],
        out_specs=pl.BlockSpec((1, rows, wide), lambda i: (i, 0, 0)),
        out_shape=jax.ShapeDtypeStruct((len(plans), rows, wide), bf16),
        compiler_params=pltpu.CompilerParams(dimension_semantics=("arbitrary",)),
        cost_estimate=pl.CostEstimate(
            flops=0,
            bytes_accessed=2 * (sum(a.size for a in arrays) + len(plans) * rows * wide),
            transcendentals=0,
        ),
    )(*arrays)


def per_device(
    tokens,
    cotangent,
    lengths,
    routes,
    query_weight,
    key_weight,
    value_weight,
    output_weight,
    query_bias,
    key_bias,
    value_bias,
    attention_gain,
    router_weight,
    shared_switch,
    mixer_gain,
    shared_gate_weight,
    shared_up_weight,
    shared_down_weight,
    expert_gate,
    expert_up,
    expert_down,
):
    net = Links()
    across, yrows = net.across, net.rows
    dp_size = PLANES * across
    groups = yrows * PAIR
    rows = tokens.shape[1]
    width = tokens.shape[2]
    top_count = routes.shape[2]
    local_experts = expert_gate.shape[0]
    num_experts = local_experts * groups
    units = local_experts + 1
    inner = expert_gate.shape[2]
    weight_rows = expert_gate.shape[1]
    shard = query_weight.shape[0]
    head_cols = width // PLANES
    heads = head_cols // HD
    window = -(-inner // (PLANES * LANES)) * LANES
    scale = HD ** (-0.5)
    all_slots = float(groups * rows * dp_size)
    iz, ix, iy, ic = net.at["z"], net.at["x"], net.at["y"], net.at["c"]
    expert_at = iy * PAIR + ic

    tok = tokens.reshape(rows, width)
    cot = cotangent.reshape(rows, width)
    length = jnp.take(lengths, expert_at)
    own_start = (iz * across + ix) * rows
    positions = own_start + jnp.arange(rows)
    valid = positions < length
    live = valid.astype(f32)[:, None]
    token_rows = tok.astype(f32)
    grad_final = cot.astype(f32) * live

    tok_blocks = net.gather_z(tok)
    extras = jnp.concatenate(
        [
            attention_gain[:, None],
            mixer_gain[:, None],
            shared_switch[:, None],
            router_weight,
            jnp.zeros((shard, LANES - 3 - num_experts), bf16),
        ],
        axis=1,
    )

    def by_plane(w):
        return jnp.transpose(w.reshape(shard, PLANES, head_cols), (1, 0, 2))

    qkv_own = jnp.concatenate(
        [by_plane(w) for w in (query_weight, key_weight, value_weight)]
        + [jnp.broadcast_to(extras[None], (PLANES, shard, LANES))],
        axis=2,
    )
    qkv_own = net.exchange_z(qkv_own)
    starts = [min(k * window, inner - window) for k in range(PLANES)]
    routed_cut = cut_columns(
        [expert_gate, expert_up, expert_down],
        [[(k, j, s) for k in range(3) for j in range(local_experts)] for s in starts],
        window,
    )
    shared_cut = cut_columns(
        [shared_gate_weight, shared_up_weight, shared_down_weight],
        [
            [(k, None, e * inner + s) for k in range(3)]
            for s in starts
            for e in range(groups)
        ],
        window,
    )
    cot_all = lax.all_gather(after(cot, qkv_own), TILES)
    routed_own = net.exchange_z(after(routed_cut, qkv_own))
    if across == 2 and yrows == 2:
        half = PLANES // 2
        from_x = net.turn(qkv_own, "x", 1)
        from_y = net.turn(qkv_own, "y", 1)
        across_both = jnp.concatenate(
            [net.turn(from_y[:half], "x", 1), net.turn(from_x[half:], "y", 1)], axis=0
        )
        qkv_w = net.place_rows(
            [
                net.place_rows([qkv_own, from_x], "x", 1),
                net.place_rows([from_y, across_both], "x", 1),
            ],
            "y",
            2,
        )
    else:
        qkv_w = net.place_rows(net.gather_x(qkv_own), "x", 1)
        qkv_w = net.place_rows([net.turn(qkv_w, "y", t) if t else qkv_w for t in range(yrows)], "y", 2)
    qkv_w = net.place_rows([qkv_w, net.turn(qkv_w, "c", 1)], "c", 3)
    qkv_w = qkv_w.reshape(width, 3 * head_cols + LANES)
    small = qkv_w[:, 3 * head_cols :]
    qkv_w = qkv_w[:, : 3 * head_cols]
    small_rows = mm_t(jnp.eye(16, LANES, dtype=bf16), small)
    attn_gain_f = small_rows[0]
    mixer_gain_f = small_rows[1]
    switch_full = small[:, 2]
    switch_row = small_rows[2]
    router_full = small[:, 3 : 3 + num_experts]

    biases = jnp.concatenate(
        [
            query_bias[:, None],
            key_bias[:, None],
            value_bias[:, None],
            jnp.zeros((shard, LANES - 3), bf16),
        ],
        axis=1,
    )
    out_w = after(jnp.concatenate([output_weight, biases], axis=1), qkv_own)
    out_w = net.place_rows(net.gather_x(out_w), "x", 0)
    out_w = net.place_rows([out_w, net.turn(out_w, "y", 1)], "y", 1)
    out_w = net.place_rows([out_w, net.turn(out_w, "c", 1)], "c", 2)
    out_w = out_w.reshape(head_cols, width + LANES)
    bias_cols = out_w[:, width : width + 3].astype(f32)
    out_w = out_w[:, :width]
    qkv_bias = jnp.concatenate([bias_cols[:, 0], bias_cols[:, 1], bias_cols[:, 2]])

    def gather_rows(blocks):
        pairs = [
            jnp.concatenate(
                [
                    b if t == 0 else net.turn(b, "y", t)
                    for b in blocks[k : k + 2]
                    for t in range(yrows)
                ],
                axis=0,
            )
            for k in (0, 2)
        ]
        return jnp.concatenate(pairs + [net.turn(pair, "c", 1) for pair in pairs], axis=0)

    def row_sum(pair):
        total = pair[:, 0]
        for t in range(1, yrows):
            total = add_low(total, net.turn(pair[:, t], "y", -t))
        return total

    block_c = jnp.arange(PAIR)[:, None, None]
    block_z = jnp.arange(PLANES)[None, :, None]
    block_y = jnp.arange(yrows)[None, None, :]
    block_order = (
        (net.behind("z", block_z) * yrows + net.behind("y", block_y)) * PAIR
        + net.behind("c", block_c)
    ).reshape(-1)
    block_order = block_order.astype(jnp.int32)
    tile_order = (
        net.behind("c", jnp.arange(PAIR))[:, None] * PLANES
        + net.behind("z", jnp.arange(PLANES))[None, :]
    )
    tile_order = tile_order.reshape(-1).astype(jnp.int32)
    tile = yrows * rows
    places = jnp.concatenate([net.behind("x", jnp.arange(across)), iy[None]]).astype(jnp.int32)

    route_ids = routes.reshape(rows, top_count)
    chosen = (route_ids[:, :, None] == jnp.arange(num_experts)[None, None, :]) & valid[
        :, None, None
    ]
    chosen_any = jnp.sum(chosen.astype(f32), axis=1)
    counts = jnp.sum(chosen_any, axis=0)

    hidden_rows = jnp.concatenate(tok_blocks, axis=0)
    hidden_f = hidden_rows.astype(f32)
    attn_inv_group = lax.rsqrt(jnp.mean(hidden_f * hidden_f, axis=-1, keepdims=True) + epsilon)
    normed_attn = (hidden_f * attn_inv_group * attn_gain_f).astype(bf16)
    qkv_pre = mm(normed_attn, qkv_w) + qkv_bias
    planes_held = net.planes_held()
    query_pos = jnp.concatenate(
        [
            (planes_held[s] * across + ix) * rows + jnp.arange(rows)
            for s in range(PLANES)
        ]
    )
    group_rows = PLANES * rows
    cosine, sine = rope_tables(query_pos, HD)
    queries = rotate(
        qkv_pre[:, :head_cols].reshape(group_rows, heads, HD), cosine, sine
    ).astype(bf16)
    keys_own = (
        rotate(
            qkv_pre[:, head_cols : 2 * head_cols].reshape(group_rows, heads, HD), cosine, sine
        )
        .astype(bf16)
        .reshape(group_rows, head_cols)
    )
    values_own = qkv_pre[:, 2 * head_cols :].astype(bf16)
    count_rows = jnp.zeros((16, 2 * head_cols), f32).at[0, :num_experts].set(counts)
    keys_values = net.gather_x(
        jnp.concatenate(
            [
                jnp.concatenate([keys_own, values_own], axis=1),
                count_rows.astype(bf16),
            ],
            axis=0,
        )
    )
    counts_x = sum(kv[group_rows, :num_experts].astype(f32) for kv in keys_values)
    keys_values = [kv[:group_rows] for kv in keys_values]
    key_pos = jnp.concatenate(
        [query_pos + (net.behind("x", t) - ix) * rows for t in range(across)]
    )
    all_kv = jnp.concatenate(keys_values, axis=0)
    keys_all = all_kv[:, :head_cols].reshape(-1, heads, HD)
    values_all = all_kv[:, head_cols:].reshape(-1, heads, HD)
    scores = jnp.einsum("qhd,khd->hqk", queries, keys_all, preferred_element_type=f32) * scale
    allowed = (key_pos[None, :] <= query_pos[:, None]) & (key_pos[None, :] < length)
    scores = jnp.where(allowed[None], scores, neg_large)
    attn_weights = jax.nn.softmax(scores, axis=-1)
    weights_low = attn_weights.astype(bf16)
    mixed = jnp.einsum("hqk,khd->qhd", weights_low, values_all, preferred_element_type=f32)
    mixed = mixed.astype(bf16).reshape(group_rows, head_cols)
    branch = mm(mixed, out_w).astype(bf16).reshape(PLANES, rows, width)
    routed_parts = net.gather_x(after(routed_own, branch))
    resid = token_rows
    for part in net.scatter_z(*[branch[s] for s in range(PLANES)]):
        resid = resid + part.astype(f32)

    mix_inv = lax.rsqrt(jnp.mean(resid * resid, axis=-1, keepdims=True) + epsilon)
    normed_mix = (resid * mix_inv * mixer_gain_f).astype(bf16)
    logits = mm(normed_mix, router_full)
    probs = jax.nn.softmax(logits, axis=-1)
    gates = probs * chosen_any
    switch = jax.nn.sigmoid(mm(normed_mix, switch_full[:, None]))
    gate_count = num_experts + 1

    def two_parts(value):
        high = lax.reduce_precision(value, 8, 7)
        return [high.astype(bf16), (value - high).astype(bf16)]

    parts = two_parts(jnp.concatenate([gates, switch * live], axis=1))
    first_row = (jnp.arange(rows) == 0).astype(f32)[:, None]
    parts += two_parts(first_row * counts_x[None]) + two_parts(probs * live)
    extra_at = 2 * gate_count
    extra_count = 4 * num_experts
    parts.append(jnp.zeros((rows, LANES - extra_at - extra_count), bf16))
    mix_blocks = net.gather_z(jnp.concatenate([normed_mix] + parts, axis=1))
    mix_blocks = mix_blocks[:1] + [after(b, *routed_parts) for b in mix_blocks[1:]]
    shared_own = net.exchange_group(after(shared_cut, *mix_blocks))
    shared_own = shared_own.reshape(PLANES, weight_rows, 3 * window)
    shared_parts = net.gather_x(shared_own)
    mix_group = gather_rows(mix_blocks)

    block_sums = jnp.sum(
        mix_group[:, width + extra_at : width + extra_at + extra_count]
        .astype(f32)
        .reshape(PAIR * PLANES * yrows, rows, extra_count),
        axis=1,
    )
    block_sums = jnp.zeros_like(block_sums).at[block_order].set(block_sums)
    sums = jnp.sum(block_sums.reshape(-1, extra_count), axis=0, keepdims=True)
    column = jnp.arange(window)
    fresh = column + jnp.minimum(iz * window, inner - window) >= iz * window
    unit_at = jnp.concatenate(
        [
            expert_at * local_experts + jnp.arange(local_experts),
            jnp.full((1,), num_experts),
        ]
    )
    unit_at = jnp.broadcast_to(unit_at[:, None], (units, window)).reshape(-1)
    fresh = jnp.tile(fresh, units)
    lane = jnp.arange(LANES)
    lane_gate = jnp.where(lane < extra_at, lane % gate_count, -1)
    widen = ((lane_gate[:, None] == unit_at[None]) & fresh[None]).astype(bf16)
    fold = ((lane[None] == unit_at[:, None]) & fresh[:, None]).astype(bf16)
    split = local_experts * window
    routed = run_experts(
        places,
        tile_order,
        tile,
        mix_group,
        cot_all.reshape(-1, tile, width),
        widen[:, :split],
        fold[:split],
        [routed_parts],
    )
    cot_group = routed[4]
    count_all = sums[0, :num_experts] + sums[0, num_experts : 2 * num_experts]
    mass_x = sums[0, 2 * num_experts : 3 * num_experts] + sums[0, 3 * num_experts :]
    fraction = count_all / (top_count * all_slots)
    shared = run_experts(
        places,
        tile_order,
        tile,
        mix_group,
        cot_group,
        widen[:, split:],
        fold[split:],
        [shared_parts, routed_parts],
        routed[0],
        routed[1],
    )
    out_sum = lax.psum_scatter(
        shared[4].reshape(-1, rows, width), TILES, scatter_dimension=0, tiled=True
    )[0]
    back = shared[0].reshape(PAIR, PLANES, yrows, rows, -1)
    pair = add_low(back[0], net.turn(back[1], "c", 1))
    kept_far = row_sum(pair[1:3])
    kept_near = row_sum(jnp.stack([pair[0], pair[3]]))

    mix_late = after(mix_group, pair)
    (shared_term,) = run_terms(
        [[(mix_late, shared[2]), (mix_late, shared[3]), (after(cot_group, pair), shared[1])]],
        width,
        PLANES,
        across,
    )

    def over_x(term, *until):
        total = net.pick(term, ix, 0).astype(f32)
        for t in range(1, across):
            got = net.turn(net.pick(term, net.ahead("x", t), 0), "x", t)
            total = total + (after(got, *until) if until else got).astype(f32)
        return total.astype(bf16)

    shared_sent = over_x(shared_term)
    shared_sorted = net.exchange_group(shared_sent.reshape(-1, shard, 3 * window))
    mix_late = after(mix_group, shared_sent, kept_far)
    (routed_term,) = run_terms(
        [[(mix_late, routed[2]), (mix_late, routed[3]), (cot_group, routed[1])]],
        width,
        PLANES,
        across,
    )
    grad_sum = sum(
        after(part, routed_term).astype(f32)
        for part in net.scatter_z(kept_near[0], kept_far[0], kept_far[1], kept_near[1])
    )

    grad_gates = grad_sum[:, width : width + num_experts]
    grad_switch = grad_sum[:, width + num_experts : width + gate_count]
    grad_switch_logit = grad_switch * live * switch * (1.0 - switch)
    grad_probs = grad_gates * chosen_any * live + live * (num_experts * fraction / all_slots)[None, :]
    grad_logits = (
        probs * (grad_probs - jnp.sum(probs * grad_probs, axis=1, keepdims=True))
    ).astype(bf16)
    grad_normed_mix = (
        grad_sum[:, :width]
        + grad_switch_logit * switch_row[None, :]
        + mm_t(grad_logits, router_full)
    )
    grad_mix_rows, grad_mixer_gain = norm_back(grad_normed_mix, resid, mix_inv, mixer_gain_f)
    grad_resid = grad_final + grad_mix_rows
    grad_branch = grad_resid.astype(bf16)
    branch_group = jnp.concatenate(net.gather_z(grad_branch), axis=0)
    branch_group = after(branch_group, out_sum, shared_sorted)

    grad_mixed = mm_t(branch_group, out_w).astype(bf16).reshape(group_rows, heads, HD)
    grad_attn = jnp.einsum("qhd,khd->hqk", grad_mixed, values_all, preferred_element_type=f32)
    routed_sent = over_x(routed_term, grad_attn)
    routed_sorted = net.exchange_z(routed_sent)
    delta = jnp.sum(attn_weights * grad_attn, axis=-1, keepdims=True)
    grad_scores = (attn_weights * (grad_attn - delta)).astype(bf16)
    grad_keys = (
        jnp.einsum("hqk,qhd->khd", grad_scores, queries, preferred_element_type=f32) * scale
    )
    grad_values = jnp.einsum("hqk,qhd->khd", weights_low, grad_mixed, preferred_element_type=f32)
    grad_kv = jnp.concatenate(
        [grad_keys.reshape(-1, head_cols), grad_values.reshape(-1, head_cols)], axis=1
    ).reshape(across, group_rows, 2 * head_cols)
    grad_kv = after(grad_kv, routed_sent)
    grad_kv_own = grad_kv[0]
    for t in range(1, across):
        grad_kv_own = grad_kv_own + net.turn(grad_kv[t].astype(bf16), "x", -t).astype(f32)
    grad_queries = (
        jnp.einsum("hqk,khd->qhd", grad_scores, keys_all, preferred_element_type=f32) * scale
    )
    grad_query_pre = (
        rotate_back(grad_queries, cosine, sine).reshape(group_rows, head_cols).astype(bf16)
    )
    grad_key_pre = (
        rotate_back(grad_kv_own[:, :head_cols].reshape(group_rows, heads, HD), cosine, sine)
        .reshape(group_rows, head_cols)
        .astype(bf16)
    )
    grad_value_pre = grad_kv_own[:, head_cols:].astype(bf16)
    grad_qkv = jnp.concatenate([grad_query_pre, grad_key_pre, grad_value_pre], axis=1)
    def to_rows(part, dims):
        part = net.scatter_axis(part, "c", dims - 1).astype(bf16)
        cut = part.shape[-1] // (2 * LANES) * LANES
        if across > 2:
            cut = part.shape[-1]
        first = net.scatter_axis(part[..., :cut], "y", dims - 2).astype(bf16)
        first = net.scatter_axis(first, "x", dims - 3).astype(bf16)
        if cut == part.shape[-1]:
            return first
        second = net.scatter_axis(part[..., cut:], "x", dims - 3).astype(bf16)
        second = net.scatter_axis(second, "y", dims - 3).astype(bf16)
        return jnp.concatenate([first, second], axis=-1)

    row_terms = jnp.concatenate(
        [
            t_mm(grad_logits, normed_mix),
            jnp.sum(grad_switch_logit * normed_mix.astype(f32), axis=0)[None],
            grad_mixer_gain[None],
            jnp.zeros((16 - num_experts - 2, width), f32),
        ],
        axis=0,
    ).astype(bf16)
    (qkv_term,) = run_terms(
        [[(normed_attn, grad_qkv), (row_terms, jnp.eye(16, LANES, dtype=bf16))]],
        width,
        PLANES,
        across,
    )
    qkv_rows = to_rows(
        jnp.swapaxes(qkv_term.reshape(across, PLANES, yrows, PAIR, shard, -1), 0, 1),
        4,
    )
    grad_normed_part = mm_t(after(grad_qkv, qkv_term), qkv_w)
    normed_part_low = grad_normed_part.astype(bf16).reshape(PLANES, rows, width)
    grad_normed_attn = jnp.zeros((rows, width), f32)
    for part in net.scatter_z(*[normed_part_low[s] for s in range(PLANES)]):
        grad_normed_attn = grad_normed_attn + after(part, qkv_rows, routed_sorted).astype(f32)
    attn_inv = attn_inv_group[:rows]
    grad_attn_rows, _ = norm_back(grad_normed_attn, token_rows, attn_inv, attn_gain_f)
    grad_tokens = (grad_resid + grad_attn_rows).astype(bf16).reshape(1, rows, width)

    layer_out = ((resid + out_sum.astype(f32)) * live).astype(bf16)

    def unit_columns(by_plane, j):
        cols = [by_plane[k, :, j * window : (j + 1) * window] for k in range(PLANES)]
        used = window * (PLANES - 1)
        cols[-1] = cols[-1][:, window - (inner - used) :]
        return jnp.concatenate(cols, axis=1)

    def routed_grads(by_plane):
        return jnp.stack(
            [unit_columns(by_plane, j) for j in range(local_experts)]
        ).astype(f32)

    grad_expert_gate, grad_expert_up, grad_expert_down = [
        routed_grads(routed_sorted[:, :, k * split : (k + 1) * split]) for k in range(3)
    ]
    shared_back = shared_sorted.reshape(PLANES, groups, shard, 3 * window)
    shared_grads = []
    for k in range(3):
        cols = []
        for e in range(groups):
            for z in range(PLANES):
                first = k * window + (window * PLANES - inner if z == PLANES - 1 else 0)
                cols.append(shared_back[z, e, :, first : (k + 1) * window])
        shared_grads.append(jnp.concatenate(cols, axis=1).astype(f32))

    grad_out_w = t_mm(mixed, branch_group).astype(bf16)
    grad_output_weight = to_rows(
        grad_out_w.reshape(across, yrows, PAIR, shard, width), 3
    ).astype(f32)
    qkv_planes = net.exchange_z(after(qkv_rows, routed_sorted))
    grad_qkv_weights = [
        jnp.concatenate(
            [qkv_planes[k, :, j * head_cols : (j + 1) * head_cols] for k in range(PLANES)], axis=1
        ).astype(f32)
        for j in range(3)
    ]

    row_grads = jnp.sum(
        qkv_planes[:, :, 3 * head_cols : 3 * head_cols + num_experts + 2].astype(f32), axis=0
    )

    gain_grad = sum(
        jnp.sum(w.astype(f32) * g, axis=1)
        for w, g in zip((query_weight, key_weight, value_weight), grad_qkv_weights)
    ) / attention_gain.astype(f32)

    bias_part = jnp.sum(grad_qkv.astype(f32), axis=0).reshape(3, across, yrows, PAIR, shard)
    bias_part = after(bias_part, grad_normed_attn)
    bias_part = jnp.transpose(bias_part, (1, 2, 3, 0, 4))
    bias_part = net.scatter_axis(bias_part, "c", 2)
    bias_part = net.scatter_axis(bias_part, "y", 1)
    mass_row = jnp.broadcast_to(
        jnp.pad(mass_x, (0, shard - num_experts))[None, None], (across, 1, shard)
    )
    bias_part = jnp.concatenate([bias_part, mass_row], axis=1)
    bias_part = net.scatter_axis(bias_part, "x", 0)
    mass_all = bias_part[3, :num_experts]
    balance_loss = (num_experts * jnp.sum(fraction * mass_all / all_slots)).reshape(1)
    return (
        layer_out.reshape(1, rows, width),
        balance_loss,
        grad_tokens,
        grad_qkv_weights[0],
        grad_qkv_weights[1],
        grad_qkv_weights[2],
        grad_output_weight,
        bias_part[0],
        bias_part[1],
        bias_part[2],
        gain_grad,
        row_grads[:, :num_experts],
        row_grads[:, num_experts],
        row_grads[:, num_experts + 1],
        shared_grads[0],
        shared_grads[1],
        shared_grads[2],
        grad_expert_gate,
        grad_expert_up,
        grad_expert_down,
    )


def solution(mesh):
    dp_size, expert_size = mesh.devices.shape
    shape = (PLANES, dp_size // PLANES, expert_size // PAIR, PAIR)
    fine = Mesh(mesh.devices.reshape(shape), ALL)
    rows = P(("y", "c"), ("z", "x"), None)
    shard2 = P(ALL, None)
    shard1 = P(ALL)
    placed = (
        (rows, rows, P(), rows)
        + (shard2,) * 4
        + (shard1,) * 4
        + (shard2, shard1, shard1)
        + (shard2,) * 3
        + (rows,) * 3
    )
    outs = (
        (rows, P(), rows)
        + (shard2,) * 4
        + (shard1,) * 4
        + (shard2, shard1, shard1)
        + (shard2,) * 3
        + (rows,) * 3
    )
    return jax.shard_map(
        per_device, mesh=fine, in_specs=placed, out_specs=outs, check_vma=False
    )
```

```python
import jax
import jax.numpy as jnp
from jax import lax
from jax.experimental import pallas as pl
from jax.experimental.pallas import tpu as pltpu
from jax.sharding import Mesh
from jax.sharding import PartitionSpec as P

HEADS = 16
HD = 128
LANES = 128
PLANES = 4
PAIR = 2
VMEM_BYTES = 56 * 2**20
ALL = ("z", "x", "y", "c")
GROUP = ("z", "y", "c")
TILES = ("c", "z", "y")

f32 = jnp.float32
bf16 = jnp.bfloat16

epsilon = 1e-06
rope_base = 1000000.0
highest = lax.Precision.HIGHEST
neg_large = -1e30


def mm(left, right, contract=((1,), (0,))):
    return lax.dot_general(left, right, (contract, ((), ())), preferred_element_type=f32)


def mm_t(left, right):
    return mm(left, right, ((1,), (1,)))


def t_mm(left, right):
    return mm(left, right, ((0,), (0,)))


def rope_tables(positions, head_width):
    halfway = head_width // 2
    freqs = rope_base ** (-jnp.arange(halfway, dtype=f32) * 2.0 / head_width)
    angles = positions.astype(f32)[:, None] * freqs[None, :]
    angles = jnp.concatenate([angles, angles], axis=1)
    return (jnp.cos(angles), jnp.sin(angles))


def rotate(values, cosine, sine):
    halfway = values.shape[-1] // 2
    turned = jnp.concatenate([-values[..., halfway:], values[..., :halfway]], axis=-1)
    return values * cosine[:, None, :] + turned * sine[:, None, :]


def rotate_back(grads_in, cosine, sine):
    halfway = grads_in.shape[-1] // 2
    scaled = grads_in * sine[:, None, :]
    turned = jnp.concatenate([scaled[..., halfway:], -scaled[..., :halfway]], axis=-1)
    return grads_in * cosine[:, None, :] + turned


def norm_back(grad_normed, rows_in, inverse, gain):
    weighted = grad_normed * gain
    inner = jnp.sum(weighted * rows_in, axis=-1, keepdims=True)
    grad_rows = inverse * weighted - rows_in * inverse**3 * inner / rows_in.shape[-1]
    grad_gain = jnp.sum(grad_normed * rows_in * inverse, axis=0)
    return (grad_rows, grad_gain)


def add_low(*parts):
    total = parts[0].astype(f32)
    for part in parts[1:]:
        total = total + part.astype(f32)
    return total.astype(bf16)


class Links:
    def __init__(self):
        self.sizes = {axis: lax.axis_size(axis) for axis in ALL}
        self.at = {axis: lax.axis_index(axis) for axis in ALL}
        self.across = self.sizes["x"]
        self.rows = self.sizes["y"]

    def turn(self, value, axis, steps):
        size = self.sizes[axis]
        return lax.ppermute(value, axis, [(i, (i + steps) % size) for i in range(size)])

    def line(self, value, *pairs):
        return lax.ppermute(value, "z", pairs)

    def behind(self, axis, steps):
        return (self.at[axis] - steps) % self.sizes[axis]

    def ahead(self, axis, steps):
        return (self.at[axis] + steps) % self.sizes[axis]

    def planes_held(self):
        return self.behind("z", jnp.arange(PLANES))

    def gather_z(self, value):
        return [value] + [self.turn(value, "z", k) for k in range(1, PLANES)]

    def scatter_z(self, *blocks):
        return [blocks[0]] + [self.turn(blocks[k], "z", -k) for k in range(1, PLANES)]

    def gather_x(self, value):
        return [value] + [self.turn(value, "x", t) for t in range(1, self.across)]

    def exchange_z(self, value):
        return lax.all_to_all(value, "z", split_axis=0, concat_axis=0, tiled=True)

    def place_rows(self, blocks, axis, dim):
        shape = blocks[0].shape[:dim] + (self.sizes[axis],) + blocks[0].shape[dim:]
        buffer = jnp.zeros(shape, blocks[0].dtype)
        for s, block in enumerate(blocks):
            buffer = lax.dynamic_update_slice_in_dim(
                buffer, jnp.expand_dims(block, dim), self.behind(axis, s), dim
            )
        return buffer

    def pick(self, value, index, dim):
        return lax.dynamic_index_in_dim(value, index, dim, keepdims=False)

    def scatter_axis(self, value, axis, dim):
        total = self.pick(value, self.at[axis], dim).astype(f32)
        for s in range(1, self.sizes[axis]):
            total = total + self.turn(
                self.pick(value, self.ahead(axis, s), dim), axis, s
            ).astype(f32)
        return total

    def exchange_group(self, value):
        return lax.all_to_all(value, GROUP, split_axis=0, concat_axis=0, tiled=True)


def after(value, *others):
    return lax.optimization_barrier((value,) + others)[0]


def weight_copies(places_ref, pieces, targets, sems):
    made = []
    across = len(pieces[0])
    for per_weight, target in zip(pieces, targets):
        cols = target.shape[1]
        for t, (source, first) in enumerate(per_weight):
            planes, block = source.shape[:2]
            for z in range(planes):
                row = pl.multiple_of((z * across + places_ref[t]) * block, block)
                view = source.at[z, :, pl.ds(first, cols)]
                made.append(
                    pltpu.make_async_copy(
                        view, target.at[pl.ds(row, block)], sems.at[len(made)]
                    )
                )
    return made


def load_weights(places_ref, pieces, targets, sems):
    @pl.when(pl.program_id(0) == 0)
    def _():
        for copy in weight_copies(places_ref, pieces, targets, sems):
            copy.start()
        for copy in weight_copies(places_ref, pieces, targets, sems):
            copy.wait()


def expert_kernel(second, across, places_ref, order_ref, rows_ref, cot_ref, widen_ref, fold_ref, *refs):
    tile = rows_ref.shape[0]
    half = tile // 2
    own_at = pl.multiple_of(places_ref[across] * half, half)
    other_at = pl.multiple_of(half - own_at, half)
    if second:
        carry_ref, first_ref, refs = refs[0], refs[1], refs[2:]
    count = 2 * across if second else across
    outs, scratch = refs[count : count + 5], refs[count + 5 :]
    wide = scratch[0].shape[1]
    pieces = [[(source, k * wide) for source in refs[:across]] for k in range(3)]
    if second:
        pieces.append([(source, 2 * first_ref.shape[1]) for source in refs[across:count]])
    back_ref, hidden_ref, grad_gate_ref, grad_up_ref, last_ref = outs
    gate_w, up_w, down_w = scratch[:3]
    load_weights(places_ref, pieces, scratch[:-1], scratch[-1])
    if second:
        cot = cot_ref[...]
    else:
        cot = jnp.concatenate(
            [cot_ref[0, pl.ds(own_at, half)], cot_ref[0, pl.ds(other_at, half)]], axis=0
        )
        last_ref[...] = cot
    width = cot.shape[1]
    payload = rows_ref[...]
    rows = payload[:, :width]
    wide_gate = mm(payload[:, width:], widen_ref[...])
    gate = mm(rows, gate_w[...])
    up = mm(rows, up_w[...])
    grad_hidden = mm(cot, down_w[...])
    sigma = 1.0 / (1.0 + jnp.exp(-gate))
    act = gate * sigma
    hidden = act * up
    hidden_gated = (hidden * wide_gate).astype(bf16)
    hidden_ref[...] = hidden_gated
    tail = mm((hidden * grad_hidden).astype(bf16), fold_ref[...])
    grad_hidden = grad_hidden * wide_gate
    grad_gate = (grad_hidden * up * (sigma * (1.0 + gate * (1.0 - sigma)))).astype(bf16)
    grad_up = (grad_hidden * act).astype(bf16)
    grad_gate_ref[...] = grad_gate
    grad_up_ref[...] = grad_up
    back = mm_t(grad_gate, gate_w[...]) + mm_t(grad_up, up_w[...])
    if second:
        back = back + carry_ref[:, :width].astype(f32)
        tail = tail + carry_ref[:, width:].astype(f32)
        out = mm_t(first_ref[...], scratch[3][...]) + mm_t(hidden_gated, down_w[...])
        last_ref[0, pl.ds(own_at, half)] = out[:half].astype(bf16)
        last_ref[0, pl.ds(other_at, half)] = out[half:].astype(bf16)
    back_ref[:, :width] = back.astype(bf16)
    back_ref[:, width:] = tail.astype(bf16)


def run_experts(places, order, tile, rows, cot, widen, fold, weights, carry=None, first=None):
    second = carry is not None
    across = len(weights[0])
    flat = [piece for per_weight in weights for piece in per_weight]
    planes = flat[0].shape[0]
    wide = widen.shape[1]
    count, full = rows.shape
    width = cot.shape[-1]

    def row_block(cols):
        return pl.BlockSpec((tile, cols), lambda i, p, o: (i, 0))

    def whole(a):
        return pl.BlockSpec(a.shape, lambda i, p, o: (0, 0))

    placed = pl.BlockSpec((1, tile, width), lambda i, p, o: (o[i], 0, 0))
    extra = [carry, first] if second else []
    scratch = [pltpu.VMEM((width, wide), bf16)] * 3
    if second:
        scratch.append(pltpu.VMEM((width, first.shape[1]), bf16))
    return pl.pallas_call(
        lambda *refs: expert_kernel(second, across, *refs),
        grid_spec=pltpu.PrefetchScalarGridSpec(
            num_scalar_prefetch=2,
            grid=(count // tile,),
            in_specs=[
                row_block(full),
                row_block(width) if second else placed,
                whole(widen),
                whole(fold),
            ]
            + [row_block(a.shape[1]) for a in extra]
            + [pl.BlockSpec(memory_space=pl.ANY)] * len(flat),
            out_specs=[row_block(full)]
            + [row_block(wide)] * 3
            + [placed if second else row_block(width)],
            scratch_shapes=scratch
            + [pltpu.SemaphoreType.DMA((len(scratch) * across * planes,))],
        ),
        out_shape=[jax.ShapeDtypeStruct((count, full), bf16)]
        + [jax.ShapeDtypeStruct((count, wide), bf16)] * 3
        + [
            jax.ShapeDtypeStruct(
                (count // tile, tile, width) if second else (count, width), bf16
            )
        ],
        compiler_params=pltpu.CompilerParams(
            vmem_limit_bytes=VMEM_BYTES, dimension_semantics=("arbitrary",)
        ),
        cost_estimate=pl.CostEstimate(
            flops=2 * count * width * wide * 5,
            bytes_accessed=3 * width * wide * 2 + count * (3 * full + 2 * width + 3 * wide) * 2,
            transcendentals=count * wide,
        ),
    )(places, order, rows, cot, widen, fold, *extra, *flat)


def term_kernel(sets, *refs):
    out_refs = refs[len(refs) - len(sets) :]
    for groups, out_ref in zip(sets, out_refs):
        side, block, cols = out_ref.shape[0], out_ref.shape[2], 0
        for left, right in groups:
            part = t_mm(refs[left][...], refs[right][...])
            wide = part.shape[1]
            out_ref[:, 0, :, cols : cols + wide] = part.astype(bf16).reshape(side, block, wide)
            cols += wide


def run_terms(sets, width, planes, across):
    block = width // (planes * across)
    side = max(1, LANES // block)
    arrays, lefts = [], set()

    def number(a):
        for k, b in enumerate(arrays):
            if a is b:
                return k
        arrays.append(a)
        return len(arrays) - 1

    numbers = [[(number(left), number(right)) for left, right in pairs] for pairs in sets]
    for pairs in numbers:
        lefts.update(left for left, _ in pairs)
    wides = [sum(right.shape[1] for _, right in pairs) for pairs in sets]
    per_plane = across // side

    def spec(k, a):
        if k in lefts:
            return pl.BlockSpec((a.shape[0], side * block), lambda i: (0, i))
        return pl.BlockSpec(a.shape, lambda i: (0, 0))

    flops = sum(2 * l.shape[0] * width * r.shape[1] for pairs in sets for l, r in pairs)
    return pl.pallas_call(
        lambda *refs: term_kernel(numbers, *refs),
        grid=(planes * across // side,),
        in_specs=[spec(k, a) for k, a in enumerate(arrays)],
        out_specs=[
            pl.BlockSpec((side, 1, block, wide), lambda i: (i % per_plane, i // per_plane, 0, 0))
            for wide in wides
        ],
        out_shape=[jax.ShapeDtypeStruct((across, planes, block, wide), bf16) for wide in wides],
        compiler_params=pltpu.CompilerParams(
            vmem_limit_bytes=VMEM_BYTES, dimension_semantics=("arbitrary",)
        ),
        cost_estimate=pl.CostEstimate(
            flops=flops,
            bytes_accessed=sum(a.size * 2 for a in arrays) + width * sum(wides) * 2,
            transcendentals=0,
        ),
    )(*arrays)


def cut_kernel(plans, window, *refs):
    out_ref = refs[-1]
    for k, plan in enumerate(plans):

        @pl.when(pl.program_id(0) == k)
        def _(plan=plan):
            for j, (source, lead, start) in enumerate(plan):
                ref = refs[source]
                cols = slice(start, start + window)
                block = ref[:, cols] if lead is None else ref[lead, :, cols]
                out_ref[0, :, j * window : (j + 1) * window] = block


def cut_columns(arrays, plans, window):
    rows = arrays[0].shape[-2]
    wide = len(plans[0]) * window

    def whole(a):
        return pl.BlockSpec(a.shape, lambda i, n=a.ndim: (0,) * n)

    return pl.pallas_call(
        lambda *refs: cut_kernel(plans, window, *refs),
        grid=(len(plans),),
        in_specs=[whole(a) for a in arrays],
        out_specs=pl.BlockSpec((1, rows, wide), lambda i: (i, 0, 0)),
        out_shape=jax.ShapeDtypeStruct((len(plans), rows, wide), bf16),
        compiler_params=pltpu.CompilerParams(dimension_semantics=("arbitrary",)),
        cost_estimate=pl.CostEstimate(
            flops=0,
            bytes_accessed=2 * (sum(a.size for a in arrays) + len(plans) * rows * wide),
            transcendentals=0,
        ),
    )(*arrays)


def per_device(
    tokens,
    cotangent,
    lengths,
    routes,
    query_weight,
    key_weight,
    value_weight,
    output_weight,
    query_bias,
    key_bias,
    value_bias,
    attention_gain,
    router_weight,
    shared_switch,
    mixer_gain,
    shared_gate_weight,
    shared_up_weight,
    shared_down_weight,
    expert_gate,
    expert_up,
    expert_down,
):
    net = Links()
    across, yrows = net.across, net.rows
    dp_size = PLANES * across
    groups = yrows * PAIR
    rows = tokens.shape[1]
    width = tokens.shape[2]
    top_count = routes.shape[2]
    local_experts = expert_gate.shape[0]
    num_experts = local_experts * groups
    units = local_experts + 1
    inner = expert_gate.shape[2]
    weight_rows = expert_gate.shape[1]
    shard = query_weight.shape[0]
    head_cols = width // PLANES
    heads = head_cols // HD
    window = -(-inner // (PLANES * LANES)) * LANES
    scale = HD ** (-0.5)
    all_slots = float(groups * rows * dp_size)
    iz, ix, iy, ic = net.at["z"], net.at["x"], net.at["y"], net.at["c"]
    expert_at = iy * PAIR + ic

    tok = tokens.reshape(rows, width)
    cot = cotangent.reshape(rows, width)
    length = jnp.take(lengths, expert_at)
    own_start = (iz * across + ix) * rows
    positions = own_start + jnp.arange(rows)
    valid = positions < length
    live = valid.astype(f32)[:, None]
    token_rows = tok.astype(f32)
    grad_final = cot.astype(f32) * live

    tok_blocks = net.gather_z(tok)
    extras = jnp.concatenate(
        [
            attention_gain[:, None],
            mixer_gain[:, None],
            shared_switch[:, None],
            router_weight,
            jnp.zeros((shard, LANES - 3 - num_experts), bf16),
        ],
        axis=1,
    )

    def by_plane(w):
        return jnp.transpose(w.reshape(shard, PLANES, head_cols), (1, 0, 2))

    qkv_own = jnp.concatenate(
        [by_plane(w) for w in (query_weight, key_weight, value_weight)]
        + [jnp.broadcast_to(extras[None], (PLANES, shard, LANES))],
        axis=2,
    )
    qkv_own = net.exchange_z(qkv_own)
    starts = [min(k * window, inner - window) for k in range(PLANES)]
    routed_cut = cut_columns(
        [expert_gate, expert_up, expert_down],
        [[(k, j, s) for k in range(3) for j in range(local_experts)] for s in starts],
        window,
    )
    shared_cut = cut_columns(
        [shared_gate_weight, shared_up_weight, shared_down_weight],
        [
            [(k, None, e * inner + s) for k in range(3)]
            for s in starts
            for e in range(groups)
        ],
        window,
    )
    cot_all = lax.all_gather(after(cot, qkv_own), TILES)
    routed_own = net.exchange_z(after(routed_cut, qkv_own))
    if across == 2 and yrows == 2:
        half = PLANES // 2
        from_x = net.turn(qkv_own, "x", 1)
        from_y = net.turn(qkv_own, "y", 1)
        across_both = jnp.concatenate(
            [net.turn(from_y[:half], "x", 1), net.turn(from_x[half:], "y", 1)], axis=0
        )
        qkv_w = net.place_rows(
            [
                net.place_rows([qkv_own, from_x], "x", 1),
                net.place_rows([from_y, across_both], "x", 1),
            ],
            "y",
            2,
        )
    else:
        qkv_w = net.place_rows(net.gather_x(qkv_own), "x", 1)
        qkv_w = net.place_rows([net.turn(qkv_w, "y", t) if t else qkv_w for t in range(yrows)], "y", 2)
    qkv_w = net.place_rows([qkv_w, net.turn(qkv_w, "c", 1)], "c", 3)
    qkv_w = qkv_w.reshape(width, 3 * head_cols + LANES)
    small = qkv_w[:, 3 * head_cols :]
    qkv_w = qkv_w[:, : 3 * head_cols]
    small_rows = mm_t(jnp.eye(16, LANES, dtype=bf16), small)
    attn_gain_f = small_rows[0]
    mixer_gain_f = small_rows[1]
    switch_full = small[:, 2]
    switch_row = small_rows[2]
    router_full = small[:, 3 : 3 + num_experts]

    biases = jnp.concatenate(
        [
            query_bias[:, None],
            key_bias[:, None],
            value_bias[:, None],
            jnp.zeros((shard, LANES - 3), bf16),
        ],
        axis=1,
    )
    out_w = after(jnp.concatenate([output_weight, biases], axis=1), qkv_own)
    out_w = net.place_rows(net.gather_x(out_w), "x", 0)
    out_w = net.place_rows([out_w, net.turn(out_w, "y", 1)], "y", 1)
    out_w = net.place_rows([out_w, net.turn(out_w, "c", 1)], "c", 2)
    out_w = out_w.reshape(head_cols, width + LANES)
    bias_cols = out_w[:, width : width + 3].astype(f32)
    out_w = out_w[:, :width]
    qkv_bias = jnp.concatenate([bias_cols[:, 0], bias_cols[:, 1], bias_cols[:, 2]])

    def gather_rows(blocks):
        pairs = [
            jnp.concatenate(
                [
                    b if t == 0 else net.turn(b, "y", t)
                    for b in blocks[k : k + 2]
                    for t in range(yrows)
                ],
                axis=0,
            )
            for k in (0, 2)
        ]
        return jnp.concatenate(pairs + [net.turn(pair, "c", 1) for pair in pairs], axis=0)

    def row_sum(pair):
        total = pair[:, 0]
        for t in range(1, yrows):
            total = add_low(total, net.turn(pair[:, t], "y", -t))
        return total

    block_c = jnp.arange(PAIR)[:, None, None]
    block_z = jnp.arange(PLANES)[None, :, None]
    block_y = jnp.arange(yrows)[None, None, :]
    block_order = (
        (net.behind("z", block_z) * yrows + net.behind("y", block_y)) * PAIR
        + net.behind("c", block_c)
    ).reshape(-1)
    block_order = block_order.astype(jnp.int32)
    tile_order = (
        net.behind("c", jnp.arange(PAIR))[:, None] * PLANES
        + net.behind("z", jnp.arange(PLANES))[None, :]
    )
    tile_order = tile_order.reshape(-1).astype(jnp.int32)
    tile = yrows * rows
    places = jnp.concatenate([net.behind("x", jnp.arange(across)), iy[None]]).astype(jnp.int32)

    route_ids = routes.reshape(rows, top_count)
    chosen = (route_ids[:, :, None] == jnp.arange(num_experts)[None, None, :]) & valid[
        :, None, None
    ]
    chosen_any = jnp.sum(chosen.astype(f32), axis=1)
    counts = jnp.sum(chosen_any, axis=0)

    hidden_rows = jnp.concatenate(tok_blocks, axis=0)
    hidden_f = hidden_rows.astype(f32)
    attn_inv_group = lax.rsqrt(jnp.mean(hidden_f * hidden_f, axis=-1, keepdims=True) + epsilon)
    normed_attn = (hidden_f * attn_inv_group * attn_gain_f).astype(bf16)
    qkv_pre = mm(normed_attn, qkv_w) + qkv_bias
    planes_held = net.planes_held()
    query_pos = jnp.concatenate(
        [
            (planes_held[s] * across + ix) * rows + jnp.arange(rows)
            for s in range(PLANES)
        ]
    )
    group_rows = PLANES * rows
    cosine, sine = rope_tables(query_pos, HD)
    queries = rotate(
        qkv_pre[:, :head_cols].reshape(group_rows, heads, HD), cosine, sine
    ).astype(bf16)
    keys_own = (
        rotate(
            qkv_pre[:, head_cols : 2 * head_cols].reshape(group_rows, heads, HD), cosine, sine
        )
        .astype(bf16)
        .reshape(group_rows, head_cols)
    )
    values_own = qkv_pre[:, 2 * head_cols :].astype(bf16)
    count_rows = jnp.zeros((16, 2 * head_cols), f32).at[0, :num_experts].set(counts)
    keys_values = net.gather_x(
        jnp.concatenate(
            [
                jnp.concatenate([keys_own, values_own], axis=1),
                count_rows.astype(bf16),
            ],
            axis=0,
        )
    )
    counts_x = sum(kv[group_rows, :num_experts].astype(f32) for kv in keys_values)
    keys_values = [kv[:group_rows] for kv in keys_values]
    key_pos = jnp.concatenate(
        [query_pos + (net.behind("x", t) - ix) * rows for t in range(across)]
    )
    all_kv = jnp.concatenate(keys_values, axis=0)
    keys_all = all_kv[:, :head_cols].reshape(-1, heads, HD)
    values_all = all_kv[:, head_cols:].reshape(-1, heads, HD)
    scores = jnp.einsum("qhd,khd->hqk", queries, keys_all, preferred_element_type=f32) * scale
    allowed = (key_pos[None, :] <= query_pos[:, None]) & (key_pos[None, :] < length)
    scores = jnp.where(allowed[None], scores, neg_large)
    attn_weights = jax.nn.softmax(scores, axis=-1)
    weights_low = attn_weights.astype(bf16)
    mixed = jnp.einsum("hqk,khd->qhd", weights_low, values_all, preferred_element_type=f32)
    mixed = mixed.astype(bf16).reshape(group_rows, head_cols)
    branch = mm(mixed, out_w).astype(bf16).reshape(PLANES, rows, width)
    routed_parts = net.gather_x(after(routed_own, branch))
    resid = token_rows
    for part in net.scatter_z(*[branch[s] for s in range(PLANES)]):
        resid = resid + part.astype(f32)

    mix_inv = lax.rsqrt(jnp.mean(resid * resid, axis=-1, keepdims=True) + epsilon)
    normed_mix = (resid * mix_inv * mixer_gain_f).astype(bf16)
    logits = mm(normed_mix, router_full)
    probs = jax.nn.softmax(logits, axis=-1)
    gates = probs * chosen_any
    switch = jax.nn.sigmoid(mm(normed_mix, switch_full[:, None]))
    gate_count = num_experts + 1

    def two_parts(value):
        high = lax.reduce_precision(value, 8, 7)
        return [high.astype(bf16), (value - high).astype(bf16)]

    parts = two_parts(jnp.concatenate([gates, switch * live], axis=1))
    first_row = (jnp.arange(rows) == 0).astype(f32)[:, None]
    parts += two_parts(first_row * counts_x[None]) + two_parts(probs * live)
    extra_at = 2 * gate_count
    extra_count = 4 * num_experts
    parts.append(jnp.zeros((rows, LANES - extra_at - extra_count), bf16))
    mix_blocks = net.gather_z(jnp.concatenate([normed_mix] + parts, axis=1))
    mix_blocks = mix_blocks[:1] + [after(b, *routed_parts) for b in mix_blocks[1:]]
    shared_own = net.exchange_group(after(shared_cut, *mix_blocks))
    shared_own = shared_own.reshape(PLANES, weight_rows, 3 * window)
    shared_parts = net.gather_x(shared_own)
    mix_group = gather_rows(mix_blocks)

    block_sums = jnp.sum(
        mix_group[:, width + extra_at : width + extra_at + extra_count]
        .astype(f32)
        .reshape(PAIR * PLANES * yrows, rows, extra_count),
        axis=1,
    )
    block_sums = jnp.zeros_like(block_sums).at[block_order].set(block_sums)
    sums = jnp.sum(block_sums.reshape(-1, extra_count), axis=0, keepdims=True)
    column = jnp.arange(window)
    fresh = column + jnp.minimum(iz * window, inner - window) >= iz * window
    unit_at = jnp.concatenate(
        [
            expert_at * local_experts + jnp.arange(local_experts),
            jnp.full((1,), num_experts),
        ]
    )
    unit_at = jnp.broadcast_to(unit_at[:, None], (units, window)).reshape(-1)
    fresh = jnp.tile(fresh, units)
    lane = jnp.arange(LANES)
    lane_gate = jnp.where(lane < extra_at, lane % gate_count, -1)
    widen = ((lane_gate[:, None] == unit_at[None]) & fresh[None]).astype(bf16)
    fold = ((lane[None] == unit_at[:, None]) & fresh[:, None]).astype(bf16)
    split = local_experts * window
    routed = run_experts(
        places,
        tile_order,
        tile,
        mix_group,
        cot_all.reshape(-1, tile, width),
        widen[:, :split],
        fold[:split],
        [routed_parts],
    )
    cot_group = routed[4]
    count_all = sums[0, :num_experts] + sums[0, num_experts : 2 * num_experts]
    mass_x = sums[0, 2 * num_experts : 3 * num_experts] + sums[0, 3 * num_experts :]
    fraction = count_all / (top_count * all_slots)
    shared = run_experts(
        places,
        tile_order,
        tile,
        mix_group,
        cot_group,
        widen[:, split:],
        fold[split:],
        [shared_parts, routed_parts],
        routed[0],
        routed[1],
    )
    out_sum = lax.psum_scatter(
        shared[4].reshape(-1, rows, width), TILES, scatter_dimension=0, tiled=True
    )[0]
    back = shared[0].reshape(PAIR, PLANES, yrows, rows, -1)
    pair = add_low(back[0], net.turn(back[1], "c", 1))
    kept_far = row_sum(pair[1:3])
    kept_near = row_sum(jnp.stack([pair[0], pair[3]]))

    mix_late = after(mix_group, pair)
    (shared_term,) = run_terms(
        [[(mix_late, shared[2]), (mix_late, shared[3]), (after(cot_group, pair), shared[1])]],
        width,
        PLANES,
        across,
    )

    def over_x(term, *until):
        total = net.pick(term, ix, 0).astype(f32)
        for t in range(1, across):
            got = net.turn(net.pick(term, net.ahead("x", t), 0), "x", t)
            total = total + (after(got, *until) if until else got).astype(f32)
        return total.astype(bf16)

    shared_sent = over_x(shared_term)
    shared_sorted = net.exchange_group(shared_sent.reshape(-1, shard, 3 * window))
    mix_late = after(mix_group, shared_sent, kept_far)
    (routed_term,) = run_terms(
        [[(mix_late, routed[2]), (mix_late, routed[3]), (cot_group, routed[1])]],
        width,
        PLANES,
        across,
    )
    grad_sum = sum(
        after(part, routed_term).astype(f32)
        for part in net.scatter_z(kept_near[0], kept_far[0], kept_far[1], kept_near[1])
    )

    grad_gates = grad_sum[:, width : width + num_experts]
    grad_switch = grad_sum[:, width + num_experts : width + gate_count]
    grad_switch_logit = grad_switch * live * switch * (1.0 - switch)
    grad_probs = grad_gates * chosen_any * live + live * (num_experts * fraction / all_slots)[None, :]
    grad_logits = (
        probs * (grad_probs - jnp.sum(probs * grad_probs, axis=1, keepdims=True))
    ).astype(bf16)
    grad_normed_mix = (
        grad_sum[:, :width]
        + grad_switch_logit * switch_row[None, :]
        + mm_t(grad_logits, router_full)
    )
    grad_mix_rows, grad_mixer_gain = norm_back(grad_normed_mix, resid, mix_inv, mixer_gain_f)
    grad_resid = grad_final + grad_mix_rows
    grad_branch = grad_resid.astype(bf16)
    branch_group = jnp.concatenate(net.gather_z(grad_branch), axis=0)
    branch_group = after(branch_group, out_sum, shared_sorted)

    grad_mixed = mm_t(branch_group, out_w).astype(bf16).reshape(group_rows, heads, HD)
    grad_attn = jnp.einsum("qhd,khd->hqk", grad_mixed, values_all, preferred_element_type=f32)
    routed_sent = over_x(routed_term, grad_attn)
    routed_sorted = net.exchange_z(routed_sent)
    delta = jnp.sum(attn_weights * grad_attn, axis=-1, keepdims=True)
    grad_scores = (attn_weights * (grad_attn - delta)).astype(bf16)
    grad_keys = (
        jnp.einsum("hqk,qhd->khd", grad_scores, queries, preferred_element_type=f32) * scale
    )
    grad_values = jnp.einsum("hqk,qhd->khd", weights_low, grad_mixed, preferred_element_type=f32)
    grad_kv = jnp.concatenate(
        [grad_keys.reshape(-1, head_cols), grad_values.reshape(-1, head_cols)], axis=1
    ).reshape(across, group_rows, 2 * head_cols)
    grad_kv = after(grad_kv, routed_sent)
    grad_kv_own = grad_kv[0]
    for t in range(1, across):
        grad_kv_own = grad_kv_own + net.turn(grad_kv[t].astype(bf16), "x", -t).astype(f32)
    grad_queries = (
        jnp.einsum("hqk,khd->qhd", grad_scores, keys_all, preferred_element_type=f32) * scale
    )
    grad_query_pre = (
        rotate_back(grad_queries, cosine, sine).reshape(group_rows, head_cols).astype(bf16)
    )
    grad_key_pre = (
        rotate_back(grad_kv_own[:, :head_cols].reshape(group_rows, heads, HD), cosine, sine)
        .reshape(group_rows, head_cols)
        .astype(bf16)
    )
    grad_value_pre = grad_kv_own[:, head_cols:].astype(bf16)
    grad_qkv = jnp.concatenate([grad_query_pre, grad_key_pre, grad_value_pre], axis=1)
    def to_rows(part, dims):
        part = net.scatter_axis(part, "c", dims - 1).astype(bf16)
        cut = part.shape[-1] // (2 * LANES) * LANES
        if across > 2:
            cut = part.shape[-1]
        first = net.scatter_axis(part[..., :cut], "y", dims - 2).astype(bf16)
        first = net.scatter_axis(first, "x", dims - 3)
        if cut == part.shape[-1]:
            return first
        second = net.scatter_axis(part[..., cut:], "x", dims - 3).astype(bf16)
        second = net.scatter_axis(second, "y", dims - 3)
        return jnp.concatenate([first, second], axis=-1)

    row_terms = jnp.concatenate(
        [
            t_mm(grad_logits, normed_mix),
            jnp.sum(grad_switch_logit * normed_mix.astype(f32), axis=0)[None],
            grad_mixer_gain[None],
            jnp.zeros((16 - num_experts - 2, width), f32),
        ],
        axis=0,
    ).astype(bf16)
    (qkv_term,) = run_terms(
        [[(normed_attn, grad_qkv), (row_terms, jnp.eye(16, LANES, dtype=bf16))]],
        width,
        PLANES,
        across,
    )
    qkv_rows = to_rows(
        jnp.swapaxes(qkv_term.reshape(across, PLANES, yrows, PAIR, shard, -1), 0, 1),
        4,
    ).astype(bf16)
    grad_normed_part = mm_t(after(grad_qkv, qkv_term), qkv_w)
    normed_part_low = grad_normed_part.astype(bf16).reshape(PLANES, rows, width)
    grad_normed_attn = jnp.zeros((rows, width), f32)
    for part in net.scatter_z(*[normed_part_low[s] for s in range(PLANES)]):
        grad_normed_attn = grad_normed_attn + after(part, qkv_rows, routed_sorted).astype(f32)
    attn_inv = attn_inv_group[:rows]
    grad_attn_rows, _ = norm_back(grad_normed_attn, token_rows, attn_inv, attn_gain_f)
    grad_tokens = (grad_resid + grad_attn_rows).astype(bf16).reshape(1, rows, width)

    layer_out = ((resid + out_sum.astype(f32)) * live).astype(bf16)

    def unit_columns(by_plane, j):
        cols = [by_plane[k, :, j * window : (j + 1) * window] for k in range(PLANES)]
        used = window * (PLANES - 1)
        cols[-1] = cols[-1][:, window - (inner - used) :]
        return jnp.concatenate(cols, axis=1)

    def routed_grads(by_plane):
        return jnp.stack(
            [unit_columns(by_plane, j) for j in range(local_experts)]
        ).astype(f32)

    grad_expert_gate, grad_expert_up, grad_expert_down = [
        routed_grads(routed_sorted[:, :, k * split : (k + 1) * split]) for k in range(3)
    ]
    shared_back = shared_sorted.reshape(PLANES, groups, shard, 3 * window)
    shared_grads = []
    for k in range(3):
        cols = []
        for e in range(groups):
            for z in range(PLANES):
                first = k * window + (window * PLANES - inner if z == PLANES - 1 else 0)
                cols.append(shared_back[z, e, :, first : (k + 1) * window])
        shared_grads.append(jnp.concatenate(cols, axis=1).astype(f32))

    spare = jnp.arange(LANES)[None, :]
    beside = sum(
        t_mm(grads, jnp.broadcast_to(spare == j, (group_rows, LANES)).astype(bf16))
        for j, grads in enumerate((grad_query_pre, grad_key_pre, grad_value_pre))
    ).astype(bf16)
    mass_parts = jnp.concatenate(
        [jnp.zeros((3,), bf16)]
        + two_parts(mass_x)
        + [jnp.zeros((LANES - 3 - 2 * num_experts,), bf16)]
    )
    beside = jnp.where(spare < 3, beside, mass_parts[None])
    grad_out_w = jnp.concatenate([t_mm(mixed, branch_group).astype(bf16), beside], axis=1)
    grad_output_weight = to_rows(
        grad_out_w.reshape(across, yrows, PAIR, shard, width + LANES), 3
    )
    bias_part = grad_output_weight[:, width : width + 3].T
    mass_all = grad_output_weight[0, width + 3 : width + 3 + 2 * num_experts]
    mass_all = (mass_all[:num_experts] + mass_all[num_experts:]) / (yrows * PAIR)
    grad_output_weight = grad_output_weight[:, :width]
    balance_loss = (num_experts * jnp.sum(fraction * mass_all / all_slots)).reshape(1)
    qkv_planes = net.exchange_z(after(qkv_rows, routed_sorted))
    grad_qkv_weights = [
        jnp.concatenate(
            [qkv_planes[k, :, j * head_cols : (j + 1) * head_cols] for k in range(PLANES)], axis=1
        ).astype(f32)
        for j in range(3)
    ]

    row_grads = jnp.sum(
        qkv_planes[:, :, 3 * head_cols : 3 * head_cols + num_experts + 2].astype(f32), axis=0
    )

    gain_grad = sum(
        jnp.sum(w.astype(f32) * g, axis=1)
        for w, g in zip((query_weight, key_weight, value_weight), grad_qkv_weights)
    ) / attention_gain.astype(f32)

    return (
        layer_out.reshape(1, rows, width),
        balance_loss,
        grad_tokens,
        grad_qkv_weights[0],
        grad_qkv_weights[1],
        grad_qkv_weights[2],
        grad_output_weight,
        bias_part[0],
        bias_part[1],
        bias_part[2],
        gain_grad,
        row_grads[:, :num_experts],
        row_grads[:, num_experts],
        row_grads[:, num_experts + 1],
        shared_grads[0],
        shared_grads[1],
        shared_grads[2],
        grad_expert_gate,
        grad_expert_up,
        grad_expert_down,
    )


def solution(mesh):
    dp_size, expert_size = mesh.devices.shape
    shape = (PLANES, dp_size // PLANES, expert_size // PAIR, PAIR)
    fine = Mesh(mesh.devices.reshape(shape), ALL)
    rows = P(("y", "c"), ("z", "x"), None)
    shard2 = P(ALL, None)
    shard1 = P(ALL)
    placed = (
        (rows, rows, P(), rows)
        + (shard2,) * 4
        + (shard1,) * 4
        + (shard2, shard1, shard1)
        + (shard2,) * 3
        + (rows,) * 3
    )
    outs = (
        (rows, P(), rows)
        + (shard2,) * 4
        + (shard1,) * 4
        + (shard2, shard1, shard1)
        + (shard2,) * 3
        + (rows,) * 3
    )
    return jax.shard_map(
        per_device, mesh=fine, in_specs=placed, out_specs=outs, check_vma=False
    )
```
